512 devices in a mesh: dom: 16 (over x, y_lo, core), shard: 32 (over y_hi, z).
Axes of the slice: x: 4, y: 4 (y_hi: 2, y_lo: 2; y = y_hi * 2 + y_lo), z: 16, core: 2. Of those that a mesh axis runs over, the one named last changes fastest.
Arguments:
- embeddings: float32 [32768, 400], P(('dom', 'shard')), may hold values from -3 to 3
- row_accum: float32 [32768], P(('dom', 'shard')), may hold values from 0.01 to 1
- relations: bfloat16 [2560, 400], replicated, may hold values from -3 to 3
- relation_accum: float32 [2560], P(('dom', 'shard')), may hold values from 0.01 to 1
- request_rows: int32 [2, 16384, 2, 16], P(None, ('dom', 'shard')), may hold values from 0 to 63
- head_slots: int32 [2, 65536], P(None, ('dom', 'shard')), may hold values from 0 to 511
- tail_slots: int32 [2, 65536], P(None, ('dom', 'shard')), may hold values from 0 to 511
- relation_ids: int32 [2, 65536], P(None, ('dom', 'shard')), may hold values from 0 to 2559
- own_negatives: int32 [2, 262144], P(None, ('dom', 'shard')), may hold values from 0 to 511
- far_negatives: int32 [2, 262144], P(None, ('dom', 'shard')), may hold values from 0 to 511
Outputs:
- new_embeddings: float32 [32768, 400], P(('dom', 'shard'))
- new_accum: float32 [32768], P(('dom', 'shard'))
- relation_step: float32 [2560, 400], P(('dom', 'shard'))
- new_relation_accum: float32 [2560], P(('dom', 'shard'))
The draws below stay inside these ranges and needn't reach their ends.
Inputs may be any that keep to these rules, and one draw needn't show every extreme that they name: `request_rows`: local row numbers within the owner's 64 rows. `head_slots`: slots of the 512 own-side touched rows. `tail_slots`: slots of the 512 partner-side touched rows. `own_negatives`: slots of the 512 own-side touched rows. `far_negatives`: slots of the 512 partner-side touched rows.
All inputs are finite; a program needn't handle non-finite values.
Results may differ from the reference program's by a relative error of at most 0.0049.
Values may be sent and summed in bfloat16 or wider, within the bound.
A program may use at most 64 MiB of HBM per device.

```python
import math
import jax
import jax.numpy as jnp
from jax import lax

D = 400
NEG = 512
ROUNDS = 2
ROWS_DEV = 64
SLOT = 16
EDGES = 128
NREL = 2560
TOUCH = 512
ENT = 32768
N_DOM = 16
N_SHARD = 32


def with_ends(result, rng, low, high):
    spot = [jax.random.randint(jax.random.fold_in(rng, axis), (), 0, length) for axis, length in enumerate(result.shape)]
    longest = result.shape.index(max(result.shape))
    neighbour = spot[:longest] + [(spot[longest] + 1) % result.shape[longest]] + spot[longest + 1:]
    return result.at[tuple(spot)].set(low).at[tuple(neighbour)].set(high)


def level_of(rng, shape, cuts, smallest, high):
    level, own = 1.0, jax.random.fold_in(rng, 6)
    for position, shards_of in cuts:
        steps = jnp.exp(jax.random.uniform(jax.random.fold_in(own, position), (shards_of,), jnp.float32, smallest / len(cuts), high / len(cuts)))
        level = level * jnp.repeat(steps, shape[position] // shards_of).reshape([-1 if axis == position else 1 for axis in range(len(shape))])
    return level


def normal_values(stream_key, shape, spread, most, shards=(), kind=jnp.bfloat16):
    values = spread * jax.random.normal(stream_key, shape, jnp.float32)
    if shards:
        values = values * level_of(stream_key, shape, shards, -0.22, 0.18)
    return jnp.clip(values, -most, most).astype(kind)


def setup_inputs(seed: int = 0) -> dict:
    arg_keys = jax.random.split(jax.random.key(seed), 11)
    embeddings = normal_values(arg_keys[0], (ENT, D), 0.5, 3.0, ((0, 512),), jnp.float32)
    row_accum = jnp.clip(jnp.exp(math.log(1.0) - 4.6051702 * jax.random.uniform(arg_keys[1], (ENT,), jnp.float32) ** level_of(arg_keys[1], (ENT,), ((0, 512),), -0.2, 0.2)), 0.01, 1.0)
    relations = normal_values(arg_keys[2], (NREL, D), 0.5, 3.0)
    relation_accum = jnp.clip(jnp.exp(math.log(1.0) - 4.6051702 * jax.random.uniform(arg_keys[3], (NREL,), jnp.float32) ** level_of(arg_keys[3], (NREL,), ((0, 512),), -0.2, 0.2)), 0.01, 1.0)
    request_rows = with_ends(jax.random.randint(arg_keys[4], (ROUNDS, N_DOM * N_SHARD * N_SHARD, 2, SLOT), 0, ROWS_DEV), jax.random.fold_in(arg_keys[4], 1), 0, ROWS_DEV - 1).astype(jnp.int32)
    head_slots = with_ends(jax.random.randint(arg_keys[5], (ROUNDS, EDGES * N_DOM * N_SHARD), 0, TOUCH), jax.random.fold_in(arg_keys[5], 1), 0, TOUCH - 1).astype(jnp.int32)
    tail_slots = with_ends(jax.random.randint(arg_keys[6], (ROUNDS, EDGES * N_DOM * N_SHARD), 0, TOUCH), jax.random.fold_in(arg_keys[6], 1), 0, TOUCH - 1).astype(jnp.int32)
    relation_ids = with_ends(jax.random.randint(arg_keys[7], (ROUNDS, EDGES * N_DOM * N_SHARD), 0, NREL), jax.random.fold_in(arg_keys[7], 1), 0, NREL - 1).astype(jnp.int32)
    own_negatives = with_ends(jax.random.randint(arg_keys[8], (ROUNDS, NEG * N_DOM * N_SHARD), 0, TOUCH), jax.random.fold_in(arg_keys[8], 1), 0, TOUCH - 1).astype(jnp.int32)
    far_negatives = with_ends(jax.random.randint(arg_keys[9], (ROUNDS, NEG * N_DOM * N_SHARD), 0, TOUCH), jax.random.fold_in(arg_keys[9], 1), 0, TOUCH - 1).astype(jnp.int32)
    return dict(embeddings=embeddings, row_accum=row_accum, relations=relations, relation_accum=relation_accum, request_rows=request_rows, head_slots=head_slots, tail_slots=tail_slots, relation_ids=relation_ids, own_negatives=own_negatives, far_negatives=far_negatives)


LEARN_RATE = 0.1

def edge_terms(own_touched, far_touched, head_slots, tail_slots, relation_ids, own_negatives, far_negatives, relations):
    neg_count = own_negatives.shape[0]
    head_vec = own_touched[head_slots].astype(jnp.float32)
    tail_vec = far_touched[tail_slots].astype(jnp.float32)
    rel_vec = relations[relation_ids].astype(jnp.float32)
    positive = lax.optimization_barrier(jnp.sum(head_vec * rel_vec * tail_vec, axis=-1))
    query_tail = (head_vec * rel_vec).astype(jnp.bfloat16)
    query_head = (tail_vec * rel_vec).astype(jnp.bfloat16)
    neg_tail = far_touched[far_negatives]
    neg_head = own_touched[own_negatives]
    contract_last = (((1,), (1,)), ((), ()))
    contract_first = (((0,), (0,)), ((), ()))
    score_tail = lax.dot_general(query_tail, neg_tail, contract_last, preferred_element_type=jnp.float32)
    score_head = lax.dot_general(query_head, neg_head, contract_last, preferred_element_type=jnp.float32)
    weight_tail = (jax.nn.sigmoid(score_tail) / neg_count).astype(jnp.bfloat16)
    weight_head = (jax.nn.sigmoid(score_head) / neg_count).astype(jnp.bfloat16)
    back_tail = jnp.dot(weight_tail, neg_tail, preferred_element_type=jnp.float32)
    back_head = jnp.dot(weight_head, neg_head, preferred_element_type=jnp.float32)
    coeff = -jax.nn.sigmoid(-positive)[:, None]
    grad_head = coeff * rel_vec * tail_vec + rel_vec * back_tail
    grad_tail = coeff * head_vec * rel_vec + rel_vec * back_head
    grad_rel = coeff * head_vec * tail_vec + head_vec * back_tail + tail_vec * back_head
    grad_negtail = lax.dot_general(weight_tail, query_tail, contract_first, preferred_element_type=jnp.float32)
    grad_neghead = lax.dot_general(weight_head, query_head, contract_first, preferred_element_type=jnp.float32)
    touch_rows = own_touched.shape[0]
    emb_width = own_touched.shape[1]
    own_grad = jnp.zeros((touch_rows, emb_width), jnp.float32).at[head_slots].add(grad_head).at[own_negatives].add(grad_neghead)
    far_grad = jnp.zeros((touch_rows, emb_width), jnp.float32).at[tail_slots].add(grad_tail).at[far_negatives].add(grad_negtail)
    return (own_grad.astype(jnp.bfloat16), far_grad.astype(jnp.bfloat16), grad_rel)

def pick_rows(table_piece, index_piece):
    return table_piece[index_piece]

def add_rows(index_piece, value_piece):
    flat_index = index_piece.reshape(-1)
    flat_value = value_piece.reshape(-1, D).astype(jnp.float32)
    return jnp.zeros((ROWS_DEV, D), jnp.float32).at[flat_index].add(flat_value)

def reference(embeddings, row_accum, relations, relation_accum, request_rows, head_slots, tail_slots, relation_ids, own_negatives, far_negatives):
    device_count = N_DOM * N_SHARD
    emb_table = embeddings.reshape(N_DOM, N_SHARD, ROWS_DEV, D)
    accum_now = row_accum.reshape(N_DOM, N_SHARD, ROWS_DEV)
    relation_grad = jnp.zeros((NREL, D), jnp.float32)
    group_index = jnp.arange(N_DOM, dtype=jnp.int32)
    for r in range(ROUNDS):
        partner = jnp.bitwise_xor(group_index, jnp.int32(1 << r))
        lowered = emb_table.astype(jnp.bfloat16)
        request_ids = request_rows[r].reshape(N_DOM, N_SHARD, N_SHARD, 2, SLOT)
        served = jax.vmap(jax.vmap(pick_rows))(lowered, request_ids)
        own_touched = served[:, :, :, 0].transpose(0, 2, 1, 3, 4).reshape(device_count, TOUCH, D)
        far_touched = served[:, :, :, 1].transpose(0, 2, 1, 3, 4)[partner].reshape(device_count, TOUCH, D)

        def device_step(carried, device_items):
            own_piece, far_piece, head_piece, tail_piece, rel_piece, own_neg, far_neg = device_items
            own_grad, far_grad, grad_rel = edge_terms(own_piece, far_piece, head_piece, tail_piece, rel_piece, own_neg, far_neg, relations)
            return (carried.at[rel_piece].add(grad_rel), (own_grad, far_grad))
        scanned = (own_touched, far_touched, head_slots[r].reshape(device_count, EDGES), tail_slots[r].reshape(device_count, EDGES), relation_ids[r].reshape(device_count, EDGES), own_negatives[r].reshape(device_count, NEG), far_negatives[r].reshape(device_count, NEG))
        relation_grad, (own_grads, far_grads) = lax.scan(device_step, relation_grad, scanned)
        own_vals = own_grads.reshape(N_DOM, N_SHARD, N_SHARD, SLOT, D).transpose(0, 2, 1, 3, 4)
        far_vals = far_grads.reshape(N_DOM, N_SHARD, N_SHARD, SLOT, D)[partner].transpose(0, 2, 1, 3, 4)
        stacked = jnp.stack([own_vals, far_vals], axis=3)
        row_grad = jax.vmap(jax.vmap(add_rows))(request_ids, stacked)
        accum_now = accum_now + lax.optimization_barrier(jnp.mean(row_grad * row_grad, axis=-1))
        emb_table = emb_table - LEARN_RATE * row_grad / jnp.sqrt(accum_now)[..., None]
    new_relation_accum = relation_accum + lax.optimization_barrier(jnp.mean(relation_grad * relation_grad, axis=-1))
    relation_step = -LEARN_RATE * relation_grad / jnp.sqrt(new_relation_accum)[:, None]
    return (emb_table.reshape(ENT, D), accum_now.reshape(ENT), relation_step, new_relation_accum)
```

```python
import jax
import jax.numpy as jnp
from jax import lax
from jax.sharding import PartitionSpec as P

LEARN_RATE = 0.1
BF = jnp.bfloat16
F32 = jnp.float32


def partner(value, axis, distance):
    mask = 2**distance
    pairs = [(source, source ^ mask) for source in range(lax.axis_size(axis))]
    return lax.ppermute(value, axis, pairs)


def mm(a, b, ca, cb):
    return lax.dot_general(a, b, (((ca,), (cb,)), ((), ())), preferred_element_type=F32)


def one_hot(ids, n):
    return (ids[:, None] == jnp.arange(n, dtype=ids.dtype)[None, :]).astype(BF)


def split_mm(a, b, ca, cb):
    hi = b.astype(BF)
    lo = (b - hi.astype(F32)).astype(BF)
    return mm(a, hi, ca, cb) + mm(a, lo, ca, cb)


def edge_terms(own, far, head_slots, tail_slots, rel_vec, own_neg, far_neg):
    touch = own.shape[0]
    neg = own_neg.shape[0]
    head_hot = one_hot(head_slots, touch)
    tail_hot = one_hot(tail_slots, touch)
    head_vec = mm(head_hot, own, 1, 0)
    tail_vec = mm(tail_hot, far, 1, 0)
    slots = jnp.arange(touch, dtype=own_neg.dtype)
    own_count = jnp.sum((own_neg[:, None] == slots[None, :]).astype(F32), axis=0)
    far_count = jnp.sum((far_neg[:, None] == slots[None, :]).astype(F32), axis=0)
    positive = jnp.sum(head_vec * rel_vec * tail_vec, axis=-1)
    query_tail = (head_vec * rel_vec).astype(BF)
    query_head = (tail_vec * rel_vec).astype(BF)
    score_tail = mm(query_tail, far, 1, 1)
    score_head = mm(query_head, own, 1, 1)
    weight_tail = (jax.nn.sigmoid(score_tail) * (far_count / neg)).astype(BF)
    weight_head = (jax.nn.sigmoid(score_head) * (own_count / neg)).astype(BF)
    back_tail = mm(weight_tail, far, 1, 0)
    back_head = mm(weight_head, own, 1, 0)
    coeff = -jax.nn.sigmoid(-positive)[:, None]
    grad_head = rel_vec * (coeff * tail_vec + back_tail)
    grad_tail = rel_vec * (coeff * head_vec + back_head)
    grad_rel = coeff * head_vec * tail_vec + head_vec * back_tail + tail_vec * back_head
    own_grad = split_mm(head_hot, grad_head, 0, 0) + mm(weight_head, query_head, 0, 0)
    far_grad = split_mm(tail_hot, grad_tail, 0, 0) + mm(weight_tail, query_tail, 0, 0)
    return own_grad.astype(BF), far_grad.astype(BF), grad_rel


def body(embeddings, row_accum, relations, relation_accum, request_rows, head_slots, tail_slots, relation_ids, own_negatives, far_negatives):
    rows, width = embeddings.shape
    shards = lax.axis_size("shard")
    slot_count = request_rows.shape[-1]
    touch = shards * slot_count
    rounds = request_rows.shape[0]
    emb = embeddings
    accum = row_accum
    rel_rows = []
    all_rel = relations[relation_ids.reshape(-1)].astype(F32).reshape(rounds, -1, width)
    for r in range(rounds):
        lowered = emb.astype(BF)
        ids = request_rows[r].reshape(-1)
        hot = one_hot(ids, rows)
        served = mm(hot, lowered, 1, 0).astype(BF).reshape(shards, 2, slot_count, width)
        received = lax.all_to_all(served, "shard", split_axis=0, concat_axis=0, tiled=True)
        own = received[:, 0].reshape(touch, width)
        far = partner(received[:, 1].reshape(touch, width), "dom", r)
        own_grad, far_grad, grad_rel = edge_terms(
            own, far, head_slots[r], tail_slots[r], all_rel[r], own_negatives[r], far_negatives[r]
        )
        rel_rows.append(grad_rel.astype(BF))
        far_back = partner(far_grad, "dom", r)
        outgoing = jnp.stack(
            [own_grad.reshape(shards, slot_count, width), far_back.reshape(shards, slot_count, width)], axis=1
        )
        returned = lax.all_to_all(outgoing, "shard", split_axis=0, concat_axis=0, tiled=True)
        row_grad = mm(hot, returned.reshape(-1, width), 0, 0)
        accum = accum + jnp.mean(row_grad * row_grad, axis=-1)
        emb = emb - LEARN_RATE * row_grad / jnp.sqrt(accum)[:, None]
    mine = jnp.concatenate(rel_rows, axis=0)
    ids = lax.all_gather(relation_ids.reshape(-1), "dom", tiled=True)
    group_rows = lax.all_gather(mine, "dom", tiled=True)
    per_group = relations.shape[0] // lax.axis_size("dom")
    local = ids - lax.axis_index("dom").astype(ids.dtype) * per_group
    dense = mm(one_hot(local, per_group), group_rows, 0, 0)
    pieces = dense.reshape(shards, per_group // shards, width)
    pieces = lax.all_to_all(pieces, "shard", split_axis=0, concat_axis=0, tiled=True)
    own_share = jnp.sum(pieces, axis=0)
    new_relation_accum = relation_accum + jnp.mean(own_share * own_share, axis=-1)
    relation_step = -LEARN_RATE * own_share / jnp.sqrt(new_relation_accum)[:, None]
    return (emb, accum, relation_step, new_relation_accum)


def solution(mesh):
    both = ("dom", "shard")
    return jax.shard_map(
        body,
        mesh=mesh,
        in_specs=(P(both, None), P(both), P(), P(both), P(None, both, None, None)) + (P(None, both),) * 5,
        out_specs=(P(both, None), P(both), P(both, None), P(both)),
        check_vma=False,
    )
```

```python
import functools

import jax
import jax.numpy as jnp
from jax import lax
from jax.experimental import pallas as pl
from jax.experimental.pallas import tpu as pltpu
from jax.sharding import PartitionSpec as P

LEARN_RATE = 0.1
BF = jnp.bfloat16
F32 = jnp.float32
MESH = pl.DeviceIdType.MESH
WIDE = 512
IDX_AT = 448
PER = 64


def mm(a, b, ca, cb):
    return lax.dot_general(a, b, (((ca,), (cb,)), ((), ())), preferred_element_type=F32)


def one_hot(ids, n):
    return (ids[:, None] == jnp.arange(n, dtype=ids.dtype)[None, :]).astype(BF)


def split_mm(a, b, ca, cb):
    hi = b.astype(BF)
    lo = (b - hi.astype(F32)).astype(BF)
    return mm(a, hi, ca, cb) + mm(a, lo, ca, cb)


def places(zs, mask):
    g = lax.axis_index("dom")
    s = lax.axis_index("shard")
    z = lax.rem(s, zs)
    yh = s // zs
    h = jnp.bitwise_xor(g, mask)
    base = yh * zs
    other = (1 - yh) * zs
    right = (g, base + lax.rem(z + 1, zs))
    left = (g, base + lax.rem(z + zs - 1, zs))
    peers = ((g, other + z), (h, s), (h, other + z))
    return z, yh, right, left, peers


def greet(devices):
    barrier = pltpu.get_barrier_semaphore()
    for device in devices:
        pl.semaphore_signal(barrier, inc=1, device_id=device, device_id_type=MESH)
    pl.semaphore_wait(barrier, len(devices))


def hops(zs):
    return ((zs // 2, zs - 1 - zs // 2), (zs - 1 - zs // 2, zs // 2))


def remote(src, dst, send, recv, device):
    return pltpu.make_async_remote_copy(
        src_ref=src, dst_ref=dst, send_sem=send, recv_sem=recv, device_id=device, device_id_type=MESH
    )


def half(ref, d, c):
    return ref.at[d, pl.ds(c * (PER // 2), PER // 2)]


def gather_kernel(zs, slot, mask, block_ref, own_ref, far_ref, idx_ref, line, picked, ring_send, ring_recv, peer_send, peer_recv, self_sem):
    z, yh, right, left, peers = places(zs, mask)
    greet((right, left) + peers)
    far_hops = hops(zs)

    def ring(direction, t, c):
        sign = -1 if direction == 0 else 1
        d_src = (sign * (t - 1)) % zs
        d_dst = (sign * t) % zs
        src = block_ref.at[pl.ds(c * (PER // 2), PER // 2)] if t == 1 else half(line, d_src, c)
        return remote(src, half(line, d_dst, c), ring_send.at[direction, t - 1, c], ring_recv.at[direction, t - 1, c], right if direction == 0 else left)

    outgoing = []

    def select(d):
        block = block_ref[...] if d == 0 else line[d]
        table = block[: zs if zs >= 16 else 16, WIDE - 128 :].astype(F32)
        rows = lax.broadcasted_iota(jnp.int32, table.shape, 0)
        ids = jnp.sum(jnp.where(rows == z, table, 0.0), axis=0, keepdims=True)
        idx_ref[d : d + 1, :] = ids
        ids = ids[:, IDX_AT - (WIDE - 128) :].astype(jnp.int32)
        hot = (lax.broadcasted_iota(jnp.int32, (PER, PER), 0) == ids).astype(BF)
        picked[d] = mm(hot, block, 0, 0).astype(BF)
        owner = yh * zs + lax.rem(z + d, zs)
        at = pl.ds(pl.multiple_of(owner * slot, slot), slot)
        mine = yh * 2 * slot
        theirs = (1 - yh) * 2 * slot
        own_copy = pltpu.make_async_copy(picked.at[d, pl.ds(mine, slot)], own_ref.at[at], self_sem)
        own_copy.start()
        for k, (start, dst) in enumerate(((theirs, own_ref), (mine + slot, far_ref), (theirs + slot, far_ref))):
            copy = remote(picked.at[d, pl.ds(start, slot)], dst.at[at], peer_send.at[k], peer_recv.at[k], peers[k])
            copy.start()

    for c in range(2):
        for direction in range(2):
            if far_hops[c][direction] >= 1:
                ring(direction, 1, c).start()
    select(0)
    for t in range(1, zs // 2 + 1):
        for c in range(2):
            for direction in range(2):
                if t <= far_hops[c][direction]:
                    ring(direction, t, c).wait_recv()
                    if t + 1 <= far_hops[c][direction]:
                        ring(direction, t + 1, c).start()
        select(zs - t)
        if t != zs // 2:
            select(t)
    for t in range(1, zs // 2 + 1):
        for c in range(2):
            for direction in range(2):
                if t <= far_hops[c][direction]:
                    ring(direction, t, c).wait_send()
    total = zs * slot
    whole = own_ref.at[pl.ds(0, total)]
    pltpu.make_async_copy(whole, whole, self_sem).wait()
    for k in range(3):
        copy = remote(whole, whole, peer_send.at[k], peer_recv.at[k], peers[k])
        copy.wait_send()
        copy.wait_recv()


def scatter_kernel(zs, slot, mask, own_ref, far_ref, idx_ref, grad_ref, got, term, sent, came, ring_send, ring_recv, peer_send, peer_recv, self_sem):
    z, yh, right, left, peers = places(zs, mask)
    greet((right, left) + peers)
    far_hops = hops(zs)
    mine = yh * 2 * slot
    theirs = (1 - yh) * 2 * slot

    def rows_of(line_yh, d):
        owner = line_yh * zs + lax.rem(z + d, zs)
        return pl.ds(pl.multiple_of(owner * slot, slot), slot)

    def exchange(d):
        return (
            pltpu.make_async_copy(own_ref.at[rows_of(yh, d)], got.at[d, pl.ds(mine, slot)], self_sem.at[d]),
            remote(own_ref.at[rows_of(1 - yh, d)], got.at[d, pl.ds(mine, slot)], peer_send.at[0], peer_recv.at[d, 0], peers[0]),
            remote(far_ref.at[rows_of(yh, d)], got.at[d, pl.ds(mine + slot, slot)], peer_send.at[1], peer_recv.at[d, 1], peers[1]),
            remote(far_ref.at[rows_of(1 - yh, d)], got.at[d, pl.ds(mine + slot, slot)], peer_send.at[2], peer_recv.at[d, 2], peers[2]),
        )

    order = []
    for t in range(zs // 2, 0, -1):
        order.append(t)
        if t != zs // 2:
            order.append(zs - t)
    order.append(0)
    for d in order:
        for copy in exchange(d):
            copy.start()

    def make_term(d):
        copies = exchange(d)
        copies[0].wait()
        for copy in copies[1:]:
            copy.wait_recv()
        ids = idx_ref[d : d + 1, IDX_AT - (WIDE - 128) :].astype(jnp.int32)
        hot = (lax.broadcasted_iota(jnp.int32, (PER, PER), 0) == ids).astype(BF)
        term[d] = mm(hot, got[d], 1, 0)

    def ring(direction, t, c):
        return remote(sent.at[direction, t - 1, c], came.at[direction, t - 1, c], ring_send.at[direction, t - 1, c], ring_recv.at[direction, t - 1, c], right if direction == 0 else left)

    made = set()
    for t in range(1, zs // 2 + 1):
        for c in range(2):
            for direction in range(2):
                count = far_hops[c][direction]
                if t > count:
                    continue
                d = count - t + 1
                d = d % zs if direction == 0 else (-d) % zs
                if d not in made:
                    make_term(d)
                    made.add(d)
                value = term[d, pl.ds(c * (PER // 2), PER // 2)]
                if t > 1:
                    ring(direction, t - 1, c).wait_recv()
                    value = value + came[direction, t - 2, c].astype(F32)
                sent[direction, t - 1, c] = value.astype(BF)
                ring(direction, t, c).start()
    make_term(0)
    for c in range(2):
        at = pl.ds(c * (PER // 2), PER // 2)
        value = term[0, at]
        for direction in range(2):
            count = far_hops[c][direction]
            if count:
                ring(direction, count, c).wait_recv()
                value = value + came[direction, count - 1, c].astype(F32)
        grad_ref[at, :] = value
    for t in range(1, zs // 2 + 1):
        for c in range(2):
            for direction in range(2):
                if t <= far_hops[c][direction]:
                    ring(direction, t, c).wait_send()
    whole = own_ref.at[pl.ds(0, zs * slot)]
    for k in range(3):
        remote(whole, whole, peer_send.at[k], peer_recv.at[0, k], peers[k]).wait_send()


VMEM_SPEC = pl.BlockSpec(memory_space=pltpu.VMEM)


def fetch(block, zs, slot, mask, cid):
    touch = 2 * zs * slot
    steps = zs // 2
    dma = pltpu.SemaphoreType.DMA
    return pl.pallas_call(
        functools.partial(gather_kernel, zs, slot, mask),
        name="fetch_rows",
        out_shape=(
            jax.ShapeDtypeStruct((touch, WIDE), BF),
            jax.ShapeDtypeStruct((touch, WIDE), BF),
            jax.ShapeDtypeStruct((zs, 128), F32),
        ),
        in_specs=[VMEM_SPEC],
        out_specs=(VMEM_SPEC,) * 3,
        scratch_shapes=[
            pltpu.VMEM((zs, PER, WIDE), BF),
            pltpu.VMEM((zs, PER, WIDE), BF),
            dma((2, steps, 2)),
            dma((2, steps, 2)),
            dma((3,)),
            dma((3,)),
            dma,
        ],
        compiler_params=pltpu.CompilerParams(collective_id=cid, has_side_effects=True),
    )(block)


def give_back(own_grad, far_grad, idx, zs, slot, mask, cid):
    steps = zs // 2
    dma = pltpu.SemaphoreType.DMA
    return pl.pallas_call(
        functools.partial(scatter_kernel, zs, slot, mask),
        name="return_grads",
        out_shape=jax.ShapeDtypeStruct((PER, WIDE), F32),
        in_specs=[VMEM_SPEC] * 3,
        out_specs=VMEM_SPEC,
        scratch_shapes=[
            pltpu.VMEM((zs, PER, WIDE), BF),
            pltpu.VMEM((zs, PER, WIDE), F32),
            pltpu.VMEM((2, steps, 2, PER // 2, WIDE), BF),
            pltpu.VMEM((2, steps, 2, PER // 2, WIDE), BF),
            dma((2, steps, 2)),
            dma((2, steps, 2)),
            dma((3,)),
            dma((zs, 3)),
            dma((zs,)),
        ],
        compiler_params=pltpu.CompilerParams(collective_id=cid, has_side_effects=True),
    )(own_grad, far_grad, idx)


def edge_terms(own, far, head_slots, tail_slots, rel_vec, own_neg, far_neg):
    touch = own.shape[0]
    neg = own_neg.shape[0]
    head_hot = one_hot(head_slots, touch)
    tail_hot = one_hot(tail_slots, touch)
    head_vec = mm(head_hot, own, 1, 0)
    tail_vec = mm(tail_hot, far, 1, 0)
    slots = jnp.arange(touch, dtype=own_neg.dtype)
    own_count = jnp.sum((own_neg[:, None] == slots[None, :]).astype(F32), axis=0)
    far_count = jnp.sum((far_neg[:, None] == slots[None, :]).astype(F32), axis=0)
    positive = jnp.sum(head_vec * rel_vec * tail_vec, axis=-1)
    query_tail = (head_vec * rel_vec).astype(BF)
    query_head = (tail_vec * rel_vec).astype(BF)
    score_tail = mm(query_tail, far, 1, 1)
    score_head = mm(query_head, own, 1, 1)
    weight_tail = (jax.nn.sigmoid(score_tail) * (far_count / neg)).astype(BF)
    weight_head = (jax.nn.sigmoid(score_head) * (own_count / neg)).astype(BF)
    back_tail = mm(weight_tail, far, 1, 0)
    back_head = mm(weight_head, own, 1, 0)
    coeff = -jax.nn.sigmoid(-positive)[:, None]
    grad_head = rel_vec * (coeff * tail_vec + back_tail)
    grad_tail = rel_vec * (coeff * head_vec + back_head)
    grad_rel = coeff * head_vec * tail_vec + head_vec * back_tail + tail_vec * back_head
    own_grad = split_mm(head_hot, grad_head, 0, 0) + mm(weight_head, query_head, 0, 0)
    far_grad = split_mm(tail_hot, grad_tail, 0, 0) + mm(weight_tail, query_tail, 0, 0)
    return own_grad.astype(BF), far_grad.astype(BF), grad_rel


def body(embeddings, row_accum, relations, relation_accum, request_rows, head_slots, tail_slots, relation_ids, own_negatives, far_negatives):
    rows, width = embeddings.shape
    shards = lax.axis_size("shard")
    slot = request_rows.shape[-1]
    zs = shards // 2
    rounds = request_rows.shape[0]
    emb = embeddings
    accum = row_accum
    rel_rows = []
    all_rel = relations[relation_ids.reshape(-1)].astype(F32).reshape(rounds, -1, width)
    all_rel = jnp.pad(all_rel, ((0, 0), (0, 0), (0, WIDE - width)))
    wanted = request_rows.reshape(rounds, 2, zs, 2 * slot).transpose(0, 2, 1, 3).reshape(rounds, zs, 4 * slot)
    wanted = jnp.pad(wanted, ((0, 0), (0, rows - zs), (IDX_AT - width, 0))).astype(BF)
    for r in range(rounds):
        block = jnp.concatenate([emb.astype(BF), wanted[r]], axis=1)
        own, far, idx = fetch(block, zs, slot, 1 << r, 2 * r)
        own_grad, far_grad, grad_rel = edge_terms(
            own, far, head_slots[r], tail_slots[r], all_rel[r], own_negatives[r], far_negatives[r]
        )
        rel_rows.append(grad_rel[:, :width].astype(BF))
        row_grad = give_back(own_grad, far_grad, idx, zs, slot, 1 << r, 2 * r + 1)[:, :width]
        accum = accum + jnp.mean(row_grad * row_grad, axis=-1)
        emb = emb - LEARN_RATE * row_grad / jnp.sqrt(accum)[:, None]
    mine = jnp.concatenate(rel_rows, axis=0)
    ids = lax.all_gather(relation_ids.reshape(-1), "dom", tiled=True)
    group_rows = lax.all_gather(mine, "dom", tiled=True)
    per_group = relations.shape[0] // lax.axis_size("dom")
    local = ids - lax.axis_index("dom").astype(ids.dtype) * per_group
    dense = mm(one_hot(local, per_group), group_rows, 0, 0)
    pieces = dense.reshape(shards, per_group // shards, width)
    pieces = lax.all_to_all(pieces, "shard", split_axis=0, concat_axis=0, tiled=True)
    own_share = jnp.sum(pieces, axis=0)
    new_relation_accum = relation_accum + jnp.mean(own_share * own_share, axis=-1)
    relation_step = -LEARN_RATE * own_share / jnp.sqrt(new_relation_accum)[:, None]
    return (emb, accum, relation_step, new_relation_accum)


def solution(mesh):
    both = ("dom", "shard")
    return jax.shard_map(
        body,
        mesh=mesh,
        in_specs=(P(both, None), P(both), P(), P(both), P(None, both, None, None)) + (P(None, both),) * 5,
        out_specs=(P(both, None), P(both), P(both, None), P(both)),
        check_vma=False,
    )
```

```python
import functools

import jax
import jax.numpy as jnp
from jax import lax
from jax.experimental import pallas as pl
from jax.experimental.pallas import tpu as pltpu
from jax.sharding import PartitionSpec as P

LEARN_RATE = 0.1
BF = jnp.bfloat16
F32 = jnp.float32
I32 = jnp.int32
MESH = pl.DeviceIdType.MESH
WIDE = 512
TAIL = WIDE - 128
MARK = 64
PER = 64
HALF = PER // 2
RELS = 5
INNER = 4


def mm(a, b, ca, cb):
    return lax.dot_general(a, b, (((ca,), (cb,)), ((), ())), preferred_element_type=F32)


def iota(shape, dim):
    return lax.broadcasted_iota(I32, shape, dim)


def hops(zs):
    return ((zs // 2, zs - 1 - zs // 2), (zs - 1 - zs // 2, zs // 2))


def remote(src, dst, send, recv, device):
    return pltpu.make_async_remote_copy(
        src_ref=src, dst_ref=dst, send_sem=send, recv_sem=recv, device_id=device, device_id_type=MESH
    )


class Place:
    def __init__(self, zs, xs):
        self.zs, self.xs = zs, xs
        g = lax.axis_index("dom")
        s = lax.axis_index("shard")
        self.g, self.s = g, s
        self.z = lax.rem(s, zs)
        self.yh = s // zs
        self.other = (1 - self.yh) * zs + self.z
        self.x = g // INNER
        self.inner = lax.rem(g, INNER)
        self.core = lax.rem(g, 2)
        self.ylo = self.inner // 2
        self.mate = g + 1 - 2 * self.core
        self.far_y = g + 2 - 4 * self.ylo

    def along_z(self, d):
        return (self.g, self.yh * self.zs + lax.rem(self.z + d, self.zs))

    def along_x(self, d):
        return (lax.rem(self.x + d, self.xs) * INNER + self.inner, self.s)

    def peers(self, r):
        h = self.mate if r == 0 else self.far_y
        return ((self.g, self.other), (h, self.s), (h, self.other))

    def everyone(self):
        return (
            [self.along_z(d) for d in range(1, self.zs)]
            + [self.along_x(d) for d in range(1, self.xs)]
            + list(self.peers(0))
            + list(self.peers(1)[1:])
        )

    def owner_rows(self, yh, d, slot):
        owner = yh * self.zs + lax.rem(self.z + d, self.zs)
        return pl.ds(pl.multiple_of(owner * slot, slot), slot)


class Ring:
    def __init__(self, place, send, recv):
        self.place, self.send, self.recv = place, send, recv
        self.count = hops(place.zs)

    def copy(self, src, dst, direction, t, c):
        return remote(
            src, dst, self.send.at[direction, t - 1, c], self.recv.at[direction, t - 1, c],
            self.place.along_z(1 if direction == 0 else self.place.zs - 1),
        )

    def each(self, t):
        for c in range(2):
            for direction in range(2):
                if t <= self.count[c][direction]:
                    yield direction, c


def piece(ref, c):
    return ref.at[pl.ds(c * HALF, HALF)]


def fetch(place, r, slot, block, line, picked, own, far, idx, ring, peer_send, peer_recv, self_sem, prepare):
    zs, peers = place.zs, place.peers(r)

    def step(direction, t, c):
        sign = -1 if direction == 0 else 1
        src = piece(block, c) if t == 1 else piece(line.at[(sign * (t - 1)) % zs], c)
        return ring.copy(src, piece(line.at[(sign * t) % zs], c), direction, t, c)

    def select(d):
        value = block[...] if d == 0 else line[d]
        table = value[:16, TAIL:].astype(F32)
        ids = jnp.sum(jnp.where(iota(table.shape, 0) == place.z, table, 0.0), axis=0, keepdims=True)
        idx[d : d + 1, :] = ids
        hot = (iota((PER, PER), 0) == ids[:, MARK:].astype(I32)).astype(BF)
        picked[d] = mm(hot, value, 0, 0).astype(BF)
        at = place.owner_rows(place.yh, d, slot)
        mine = place.yh * 2 * slot
        theirs = (1 - place.yh) * 2 * slot
        pltpu.make_async_copy(picked.at[d, pl.ds(mine, slot)], own.at[at], self_sem).start()
        for k, (start, dst) in enumerate(((theirs, own), (mine + slot, far), (theirs + slot, far))):
            remote(picked.at[d, pl.ds(start, slot)], dst.at[at], peer_send.at[k], peer_recv.at[k], peers[k]).start()

    for direction, c in ring.each(1):
        step(direction, 1, c).start()
    select(0)
    prepare()
    for t in range(1, zs // 2 + 1):
        for direction, c in ring.each(t):
            step(direction, t, c).wait_recv()
            if t + 1 <= ring.count[c][direction]:
                step(direction, t + 1, c).start()
        select(zs - t)
        if t != zs // 2:
            select(t)
    for t in range(1, zs // 2 + 1):
        for direction, c in ring.each(t):
            step(direction, t, c).wait_send()
    whole = own.at[pl.ds(0, zs * slot)]
    pltpu.make_async_copy(whole, whole, self_sem).wait()
    for k in range(3):
        copy = remote(whole, whole, peer_send.at[k], peer_recv.at[k], peers[k])
        copy.wait_send()
        copy.wait_recv()


def give_back(place, r, slot, own, far, idx, got, term, sent, came, ring, peer_send, peer_recv, self_sem, aside):
    zs, peers = place.zs, place.peers(r)
    mine = place.yh * 2 * slot

    def exchange(d):
        here, there = place.owner_rows(place.yh, d, slot), place.owner_rows(1 - place.yh, d, slot)
        k0, k1 = got.at[d, pl.ds(mine, slot)], got.at[d, pl.ds(mine + slot, slot)]
        return (
            pltpu.make_async_copy(own.at[here], k0, self_sem.at[d]),
            remote(own.at[there], k0, peer_send.at[0], peer_recv.at[d, 0], peers[0]),
            remote(far.at[here], k1, peer_send.at[1], peer_recv.at[d, 1], peers[1]),
            remote(far.at[there], k1, peer_send.at[2], peer_recv.at[d, 2], peers[2]),
        )

    def step(direction, t, c):
        return ring.copy(sent.at[direction, t - 1, c], came.at[direction, t - 1, c], direction, t, c)

    def make_term(d):
        copies = exchange(d)
        copies[0].wait()
        for copy in copies[1:]:
            copy.wait_recv()
        hot = (iota((PER, PER), 0) == idx[d : d + 1, MARK:].astype(I32)).astype(BF)
        term[d] = mm(hot, got[d], 1, 0)

    for t in range(zs // 2, 0, -1):
        for d in (t,) if t == zs // 2 else (t, zs - t):
            for copy in exchange(d):
                copy.start()
    for copy in exchange(0):
        copy.start()
    aside[0]()
    made = set()
    for t in range(1, zs // 2 + 1):
        for direction, c in ring.each(t):
            d = ring.count[c][direction] - t + 1
            d = d % zs if direction == 0 else (-d) % zs
            if d not in made:
                make_term(d)
                made.add(d)
            value = term[d, pl.ds(c * HALF, HALF)]
            if t > 1:
                step(direction, t - 1, c).wait_recv()
                value = value + came[direction, t - 2, c].astype(F32)
            sent[direction, t - 1, c] = value.astype(BF)
            step(direction, t, c).start()
        if t in aside:
            aside[t]()
    make_term(0)
    halves = []
    for c in range(2):
        value = term[0, pl.ds(c * HALF, HALF)]
        for direction in range(2):
            count = ring.count[c][direction]
            if count:
                step(direction, count, c).wait_recv()
                value = value + came[direction, count - 1, c].astype(F32)
        halves.append(value)
    for t in range(1, zs // 2 + 1):
        for direction, c in ring.each(t):
            step(direction, t, c).wait_send()
    whole = own.at[pl.ds(0, zs * slot)]
    for k in range(3):
        remote(whole, whole, peer_send.at[k], peer_recv.at[0, k], peers[k]).wait_send()
    return jnp.concatenate(halves, axis=0)


def main_kernel(zs, xs, slot, width, names, *refs):
    n = dict(zip(names, refs))
    place = Place(zs, xs)
    touch = 2 * zs * slot
    edges = n["edge_slots"].shape[1]
    nrel = n["rel_table"].shape[0]
    seg = zs * RELS

    table_copy = pltpu.make_async_copy(n["relations"], n["rel_table"], n["table_sem"])
    table_copy.start()
    barrier = pltpu.get_barrier_semaphore()
    everyone = place.everyone()
    for device in everyone:
        pl.semaphore_signal(barrier, inc=1, device_id=device, device_id_type=MESH)
    emb, rel_vec = n["emb"], n["rel_vec"]
    emb[...] = jnp.zeros_like(emb)
    rel_vec[...] = jnp.zeros_like(rel_vec)
    emb[:, :width] = n["emb_in"][...]
    n["accum_out"][...] = n["accum_in"][...]
    lane = iota((PER, 128), 1)

    def write_block(r):
        value = emb[...]
        block = n["block"].at[r]
        block[:, :TAIL] = value[:, :TAIL].astype(BF)
        block[:, TAIL:] = jnp.where(lane < width - TAIL, value[:, TAIL:], n["wanted"][r]).astype(BF)

    write_block(0)
    pl.semaphore_wait(barrier, len(everyone))

    def counts(row):
        neg = n["negatives"].shape[1]
        hot = (iota((touch, neg), 0) == n["negatives"][row : row + 1, :]).astype(BF)
        return mm(jnp.ones((8, neg), BF), hot, 1, 1)[:1] * (1.0 / neg)

    def prepare(r):
        if r == 0:
            table_copy.wait()
        hot = (iota((nrel, edges), 0) == n["rel_ids"][r : r + 1, :]).astype(BF)
        rel_vec[r, :, :width] = mm(hot, n["rel_table"][...], 0, 0)
        for side in range(2):
            n["count"][2 * r + side : 2 * r + side + 1, :] = counts(2 * r + side)

    def edge_step(r):
        own, far = n["own"][r], n["far"][r]
        head_hot = (iota((touch, edges), 0) == n["edge_slots"][2 * r : 2 * r + 1, :]).astype(BF)
        tail_hot = (iota((touch, edges), 0) == n["edge_slots"][2 * r + 1 : 2 * r + 2, :]).astype(BF)
        rel = rel_vec[r]
        head_vec = mm(head_hot, own, 0, 0)
        tail_vec = mm(tail_hot, far, 0, 0)
        positive = jnp.sum(head_vec * rel * tail_vec, axis=-1, keepdims=True)
        query_tail = (head_vec * rel).astype(BF)
        query_head = (tail_vec * rel).astype(BF)
        own_count = n["count"][2 * r : 2 * r + 1, :]
        far_count = n["count"][2 * r + 1 : 2 * r + 2, :]
        weight_tail = (jax.nn.sigmoid(mm(query_tail, far, 1, 1)) * far_count).astype(BF)
        weight_head = (jax.nn.sigmoid(mm(query_head, own, 1, 1)) * own_count).astype(BF)
        back_tail = mm(weight_tail, far, 1, 0)
        back_head = mm(weight_head, own, 1, 0)
        coeff = -jax.nn.sigmoid(-positive)

        def spread(hot, grad, weight, query):
            hi = grad.astype(BF)
            lo = (grad - hi.astype(F32)).astype(BF)
            return (mm(hot, hi, 1, 0) + mm(hot, lo, 1, 0) + mm(weight, query, 0, 0)).astype(BF)

        n["own_grad"][r] = spread(head_hot, rel * (coeff * tail_vec + back_tail), weight_head, query_head)
        n["far_grad"][r] = spread(tail_hot, rel * (coeff * head_vec + back_head), weight_tail, query_tail)
        grad_rel = coeff * head_vec * tail_vec + head_vec * back_tail + tail_vec * back_head
        rows = n["rows"].at[r, 0, pl.ds(0, edges)]
        rows[:, :TAIL] = grad_rel[:, :TAIL].astype(BF)
        rows[:, TAIL:] = jnp.where(iota((edges, 128), 1) < width - TAIL, grad_rel[:, TAIL:], n["rel_marks"][r]).astype(BF)

    def update(row_grad):
        accum = n["accum_out"][...] + jnp.sum(row_grad * row_grad, axis=-1, keepdims=True) * (1.0 / width)
        n["accum_out"][...] = accum
        emb[...] = emb[...] - LEARN_RATE * row_grad / jnp.sqrt(accum)

    def slot_rows(r, near, d):
        return n["rows"].at[r, near, pl.ds(d * edges, edges)]

    def x_copy(r, e):
        return remote(slot_rows(r, 0, 0), slot_rows(r, 0, e), n["x_send"].at[r, e], n["x_recv"].at[r, e], place.along_x(xs - e))

    def core_copy(r, d):
        return remote(slot_rows(r, 0, d), slot_rows(r, 1, d), n["core_send"].at[r, d], n["core_recv"].at[r, d], (place.mate, place.s))

    def rows_start(r):
        for e in range(1, xs):
            x_copy(r, e).start()
        core_copy(r, 0).start()

    def rows_forward(r):
        for e in range(1, xs):
            x_copy(r, e).wait_recv()
            core_copy(r, e).start()

    def rows_sum(r):
        for d in range(xs):
            core_copy(r, d).wait_recv()
        base = (place.x * INNER + place.core) * (2 * seg)
        total = n["dense"][...] if r else jnp.zeros((4 * seg, WIDE), F32)
        for near in range(2):
            block = n["rows"][r, near]
            marks = block[:, TAIL:].astype(F32)
            at = iota(marks.shape, 1)
            ids = jnp.sum(jnp.where(at == MARK, marks * 64.0, jnp.where(at == MARK + 1, marks, 0.0)), axis=1, keepdims=True)
            col = iota((xs * edges, 4 * seg), 1)
            target = base + col + jnp.where(col >= 2 * seg, 2 * seg, 0)
            total = total + mm((ids.astype(I32) == target).astype(BF), block, 0, 0)
        n["dense"][...] = total
        for e in range(1, xs):
            x_copy(r, e).wait_send()
        for d in range(xs):
            core_copy(r, d).wait_send()

    def seg_rows(ylo, yh):
        return pl.ds(pl.multiple_of((ylo * 2 + yh) * seg, seg), seg)

    def y_copy(k):
        ylo = place.ylo if k == 0 else 1 - place.ylo
        yh = place.yh if k == 1 else 1 - place.yh
        return remote(n["y_out"].at[seg_rows(ylo, yh)], n["y_in"].at[k], n["y_send"].at[k], n["y_recv"].at[k], place.peers(1)[k])

    def y_start():
        n["y_out"][...] = n["dense"][...].astype(BF)
        for k in range(3):
            y_copy(k).start()

    def z_copy(e):
        src = n["z_out"].at[lax.rem(place.z + zs - e, zs)]
        return remote(src, n["z_in"].at[e], n["z_send"].at[e], n["z_recv"].at[e], place.along_z(zs - e))

    def z_start():
        total = n["dense"][seg_rows(place.ylo, place.yh), :]
        for k in range(3):
            y_copy(k).wait_recv()
            total = total + n["y_in"][k].astype(F32)
        total = total.astype(BF)
        row, col = iota((zs * 16, seg), 0), iota((zs * 16, seg), 1)
        zz, k = row >> 4, row & 15
        packed = jnp.zeros((zs * 16, 128), F32)
        full = TAIL // 128
        for c in range(full):
            j = k - c * RELS
            hot = ((col == zz * RELS + j) & (j >= 0) & (j < RELS)).astype(BF)
            packed = packed + mm(hot, total[:, c * 128 : (c + 1) * 128], 1, 0)
        rest = width - TAIL
        last = total[:, TAIL:].astype(F32)
        last = jnp.where(iota(last.shape, 1) < rest, last, 0.0)
        for j in range(RELS):
            hot = ((col == zz * RELS + j) & (k == full * RELS)).astype(BF)
            moved = last if j == 0 else pltpu.roll(last, j * rest, 1)
            packed = packed + mm(hot, moved.astype(BF), 1, 0)
        packed = packed.astype(BF)
        for zz in range(zs):
            n["z_out"][zz] = packed[zz * 16 : (zz + 1) * 16]
        for e in range(1, zs):
            z_copy(e).start()

    def z_end():
        total = n["z_out"][place.z].astype(F32)
        for e in range(1, zs):
            z_copy(e).wait_recv()
            total = total + n["z_in"][e].astype(F32)
        n["rel_out"][...] = total
        for k in range(3):
            y_copy(k).wait_send()
        for e in range(1, zs):
            z_copy(e).wait_send()

    last_step = zs // 2
    for r in range(2):
        if r:
            write_block(r)
        fetch(
            place, r, slot, n["block"].at[r], n["line"].at[r], n["picked"].at[r], n["own"].at[r], n["far"].at[r], n["idx"].at[r],
            Ring(place, n["f_send"].at[r], n["f_recv"].at[r]), n["fp_send"].at[r], n["fp_recv"].at[r], n["f_self"].at[r],
            functools.partial(prepare, r),
        )
        edge_step(r)
        steps = {0: [functools.partial(rows_start, r)]}
        plan = ((2, functools.partial(rows_forward, r)), (4, functools.partial(rows_sum, r)))
        if r:
            plan = plan + ((4, y_start), (6, z_start))
        for t, what in plan:
            steps.setdefault(min(t, last_step), []).append(what)
        aside = {t: (lambda todo=todo: [f() for f in todo]) for t, todo in steps.items()}
        row_grad = give_back(
            place, r, slot, n["own_grad"].at[r], n["far_grad"].at[r], n["idx"].at[r], n["got"].at[r], n["term"], n["sent"].at[r], n["came"].at[r],
            Ring(place, n["s_send"].at[r], n["s_recv"].at[r]), n["sp_send"].at[r], n["sp_recv"].at[r], n["s_self"].at[r], aside,
        )
        update(row_grad)
    n["emb_out"][...] = emb[:, :width]
    z_end()


def run(emb, accum, relations, wanted, edge_slots, rel_ids, negatives, rel_marks, zs, xs, slot):
    width = emb.shape[1]
    touch = 2 * zs * slot
    edges = edge_slots.shape[1]
    half = zs // 2
    seg = zs * RELS
    dma = pltpu.SemaphoreType.DMA
    vmem = pltpu.VMEM
    inputs = dict(
        emb_in=emb, accum_in=accum, relations=relations, wanted=wanted, edge_slots=edge_slots, rel_ids=rel_ids,
        negatives=negatives, rel_marks=rel_marks,
    )
    outputs = dict(
        emb_out=jax.ShapeDtypeStruct(emb.shape, F32),
        accum_out=jax.ShapeDtypeStruct(accum.shape, F32),
        rel_out=jax.ShapeDtypeStruct((16, 128), F32),
    )
    scratch = dict(
        emb=vmem((PER, WIDE), F32),
        rel_table=vmem(relations.shape, BF),
        rel_vec=vmem((2, edges, WIDE), F32),
        count=vmem((4, touch), F32),
        block=vmem((2, PER, WIDE), BF),
        line=vmem((2, zs, PER, WIDE), BF),
        picked=vmem((2, zs, PER, WIDE), BF),
        own=vmem((2, touch, WIDE), BF),
        far=vmem((2, touch, WIDE), BF),
        idx=vmem((2, zs, 128), F32),
        own_grad=vmem((2, touch, WIDE), BF),
        far_grad=vmem((2, touch, WIDE), BF),
        got=vmem((2, zs, PER, WIDE), BF),
        term=vmem((zs, PER, WIDE), F32),
        sent=vmem((2, 2, half, 2, HALF, WIDE), BF),
        came=vmem((2, 2, half, 2, HALF, WIDE), BF),
        rows=vmem((2, 2, xs * edges, WIDE), BF),
        dense=vmem((4 * seg, WIDE), F32),
        y_out=vmem((4 * seg, WIDE), BF),
        y_in=vmem((3, seg, WIDE), BF),
        z_out=vmem((zs, 16, 128), BF),
        z_in=vmem((zs, 16, 128), BF),
        table_sem=dma,
        f_send=dma((2, 2, half, 2)),
        f_recv=dma((2, 2, half, 2)),
        fp_send=dma((2, 3)),
        fp_recv=dma((2, 3)),
        f_self=dma((2,)),
        s_send=dma((2, 2, half, 2)),
        s_recv=dma((2, 2, half, 2)),
        sp_send=dma((2, 3)),
        sp_recv=dma((2, zs, 3)),
        s_self=dma((2, zs)),
        x_send=dma((2, xs)),
        x_recv=dma((2, xs)),
        core_send=dma((2, xs)),
        core_recv=dma((2, xs)),
        y_send=dma((3,)),
        y_recv=dma((3,)),
        z_send=dma((zs,)),
        z_recv=dma((zs,)),
    )
    in_vmem = pl.BlockSpec(memory_space=pltpu.VMEM)
    names = (*inputs, *outputs, *scratch)
    return pl.pallas_call(
        functools.partial(main_kernel, zs, xs, slot, width, names),
        name="train_step",
        out_shape=tuple(outputs.values()),
        in_specs=[pl.BlockSpec(memory_space=pl.ANY) if k == "relations" else in_vmem for k in inputs],
        out_specs=(in_vmem,) * len(outputs),
        scratch_shapes=list(scratch.values()),
        compiler_params=pltpu.CompilerParams(collective_id=0, has_side_effects=True),
    )(*inputs.values())


def body(embeddings, row_accum, relations, relation_accum, request_rows, head_slots, tail_slots, relation_ids, own_negatives, far_negatives):
    rows, width = embeddings.shape
    slot = request_rows.shape[-1]
    zs = lax.axis_size("shard") // 2
    xs = lax.axis_size("dom") // INNER
    rounds, edges = head_slots.shape
    wanted = request_rows.reshape(rounds, 2, zs, 2 * slot).transpose(0, 2, 1, 3).reshape(rounds, zs, 4 * slot)
    wanted = jnp.pad(wanted, ((0, 0), (0, rows - zs), (MARK, 0))).astype(F32)
    marks = jnp.stack([relation_ids >> 6, relation_ids & 63], axis=-1)
    marks = jnp.pad(marks, ((0, 0), (0, 0), (MARK, 128 - MARK - 2))).astype(F32)
    edge_slots = jnp.stack([head_slots, tail_slots], axis=1).reshape(2 * rounds, edges)
    negatives = jnp.stack([own_negatives, far_negatives], axis=1).reshape(2 * rounds, -1)
    emb, accum, packed = run(
        embeddings, row_accum[:, None], relations, wanted, edge_slots, relation_ids, negatives, marks, zs, xs, slot
    )
    full, rest = width // 128, width % 128
    share = packed[: full * RELS].reshape(full, RELS, 128).transpose(1, 0, 2).reshape(RELS, full * 128)
    share = jnp.concatenate([share, packed[full * RELS, : RELS * rest].reshape(RELS, rest)], axis=1)
    new_relation_accum = relation_accum + jnp.mean(share * share, axis=-1)
    relation_step = -LEARN_RATE * share / jnp.sqrt(new_relation_accum)[:, None]
    return (emb, accum[:, 0], relation_step, new_relation_accum)


def solution(mesh):
    both = ("dom", "shard")
    return jax.shard_map(
        body,
        mesh=mesh,
        in_specs=(P(both, None), P(both), P(), P(both), P(None, both, None, None)) + (P(None, both),) * 5,
        out_specs=(P(both, None), P(both), P(both, None), P(both)),
        check_vma=False,
    )
```

```python
import functools

import jax
import jax.numpy as jnp
from jax import lax
from jax.experimental import pallas as pl
from jax.experimental.pallas import tpu as pltpu
from jax.sharding import PartitionSpec as P

LEARN_RATE = 0.1
BF = jnp.bfloat16
F32 = jnp.float32
I32 = jnp.int32
MESH = pl.DeviceIdType.MESH
WIDE = 512
TAIL = WIDE - 128
MARK = 64
PER = 64
HALF = PER // 2
RELS = 5
INNER = 4


def mm(a, b, ca, cb):
    return lax.dot_general(a, b, (((ca,), (cb,)), ((), ())), preferred_element_type=F32)


def iota(shape, dim):
    return lax.broadcasted_iota(I32, shape, dim)


def hops(zs):
    return ((zs // 2, zs - 1 - zs // 2), (zs - 1 - zs // 2, zs // 2))


def column(row, rows):
    n = row.shape[1]
    return jnp.sum(jnp.where(iota((rows, n), 0) == iota((rows, n), 1), row, jnp.zeros_like(row)), axis=1, keepdims=True)


def as_row(col, n):
    rows = col.shape[0]
    return jnp.sum(jnp.where(iota((rows, n), 0) == iota((rows, n), 1), col, jnp.zeros_like(col)), axis=0, keepdims=True)


def remote(src, dst, send, recv, device):
    return pltpu.make_async_remote_copy(
        src_ref=src, dst_ref=dst, send_sem=send, recv_sem=recv, device_id=device, device_id_type=MESH
    )


class Place:
    def __init__(self, zs, xs):
        self.zs, self.xs = zs, xs
        g = lax.axis_index("dom")
        s = lax.axis_index("shard")
        self.g, self.s = g, s
        self.z = lax.rem(s, zs)
        self.yh = s // zs
        self.other = (1 - self.yh) * zs + self.z
        self.x = g // INNER
        self.inner = lax.rem(g, INNER)
        self.core = lax.rem(g, 2)
        self.ylo = self.inner // 2
        self.mate = g + 1 - 2 * self.core
        self.far_y = g + 2 - 4 * self.ylo

    def along_z(self, d):
        return (self.g, self.yh * self.zs + lax.rem(self.z + d, self.zs))

    def along_x(self, d):
        return (lax.rem(self.x + d, self.xs) * INNER + self.inner, self.s)

    def peers(self, r):
        h = self.mate if r == 0 else self.far_y
        return ((self.g, self.other), (h, self.s), (h, self.other))

    def everyone(self):
        return (
            [self.along_z(d) for d in range(1, self.zs)]
            + [self.along_x(d) for d in range(1, self.xs)]
            + list(self.peers(0))
            + list(self.peers(1)[1:])
        )

    def owner_rows(self, yh, d, slot):
        owner = yh * self.zs + lax.rem(self.z + d, self.zs)
        return pl.ds(pl.multiple_of(owner * slot, slot), slot)


class Ring:
    def __init__(self, place, send, recv):
        self.place, self.send, self.recv = place, send, recv
        self.count = hops(place.zs)
        self.far = place.zs // 2
        self.jump = place.zs // 4 + 1
        near, rest = list(range(1, self.jump)), list(range(self.jump, self.far + 1))
        self.order = []
        while near or rest:
            for lane in (near, rest):
                if lane:
                    self.order.append(lane.pop(0))

    def copy(self, src, dst, direction, t, c, hop):
        return remote(
            src, dst, self.send.at[direction, t - 1, c], self.recv.at[direction, t - 1, c],
            self.place.along_z(hop if direction == 0 else self.place.zs - hop),
        )

    def each(self, t):
        for c in range(2):
            for direction in range(2):
                if t <= self.count[c][direction]:
                    yield direction, c


def piece(ref, c):
    return ref.at[pl.ds(c * HALF, HALF)]


def fetch(place, r, slot, block, line, picked, own, far, idx, ring, peer_send, peer_recv, self_sem):
    zs, peers = place.zs, place.peers(r)

    def step(direction, t, c):
        sign = -1 if direction == 0 else 1
        first = t in (1, ring.jump)
        src = piece(block, c) if first else piece(line.at[(sign * (t - 1)) % zs], c)
        return ring.copy(src, piece(line.at[(sign * t) % zs], c), direction, t, c, t if first else 1)

    def select(d):
        value = block[...] if d == 0 else line[d]
        table = value[:16, TAIL:].astype(F32)
        ids = jnp.sum(jnp.where(iota(table.shape, 0) == place.z, table, 0.0), axis=0, keepdims=True)
        idx[d : d + 1, :] = ids
        hot = (iota((PER, PER), 0) == ids[:, MARK:].astype(I32)).astype(BF)
        picked[d] = mm(hot, value, 0, 0).astype(BF)
        at = place.owner_rows(place.yh, d, slot)
        mine = place.yh * 2 * slot
        theirs = (1 - place.yh) * 2 * slot
        pltpu.make_async_copy(picked.at[d, pl.ds(mine, slot)], own.at[at], self_sem).start()
        for k, (start, dst) in enumerate(((theirs, own), (mine + slot, far), (theirs + slot, far))):
            remote(picked.at[d, pl.ds(start, slot)], dst.at[at], peer_send.at[k], peer_recv.at[k], peers[k]).start()

    for t in dict.fromkeys((ring.jump, 1)):
        for direction, c in ring.each(t):
            step(direction, t, c).start()
    select(0)
    for t in ring.order:
        for direction, c in ring.each(t):
            step(direction, t, c).wait_recv()
            if t + 1 <= ring.count[c][direction] and t + 1 != ring.jump:
                step(direction, t + 1, c).start()
        select(zs - t)
        if t != zs // 2:
            select(t)
    for t in range(1, zs // 2 + 1):
        for direction, c in ring.each(t):
            step(direction, t, c).wait_send()
    whole = own.at[pl.ds(0, zs * slot)]
    pltpu.make_async_copy(whole, whole, self_sem).wait()
    for k in range(3):
        copy = remote(whole, whole, peer_send.at[k], peer_recv.at[k], peers[k])
        copy.wait_send()
        copy.wait_recv()


def give_back(place, r, slot, own, far, idx, got, term, sent, came, ring, peer_send, peer_recv, self_sem, aside):
    zs, peers = place.zs, place.peers(r)
    mine = place.yh * 2 * slot

    def exchange(d):
        here, there = place.owner_rows(place.yh, d, slot), place.owner_rows(1 - place.yh, d, slot)
        k0, k1 = got.at[d, pl.ds(mine, slot)], got.at[d, pl.ds(mine + slot, slot)]
        return (
            pltpu.make_async_copy(own.at[here], k0, self_sem.at[d]),
            remote(own.at[there], k0, peer_send.at[0], peer_recv.at[d, 0], peers[0]),
            remote(far.at[here], k1, peer_send.at[1], peer_recv.at[d, 1], peers[1]),
            remote(far.at[there], k1, peer_send.at[2], peer_recv.at[d, 2], peers[2]),
        )

    def step(direction, d, c):
        hop = d if d == ring.jump else 1
        return ring.copy(sent.at[direction, d - 1, c], came.at[direction, d - 1, c], direction, d, c, hop)

    def make_term(d):
        copies = exchange(d)
        copies[0].wait()
        for copy in copies[1:]:
            copy.wait_recv()
        hot = (iota((PER, PER), 0) == idx[d : d + 1, MARK:].astype(I32)).astype(BF)
        term[d] = mm(hot, got[d], 1, 0)

    order = ring.order[::-1]
    order = sorted(order, key=lambda t: (ring.far - t) if t >= ring.jump else (ring.jump - 1 - t) + 1.5)
    for t in order:
        for d in (t,) if t == ring.far else (t, zs - t):
            for copy in exchange(d):
                copy.start()
    for copy in exchange(0):
        copy.start()
    aside[0]()
    made = set()
    for number, t in enumerate(order):
        for direction, c in ring.each(t):
            d = t if direction == 0 else zs - t
            if d not in made:
                make_term(d)
                made.add(d)
            value = term[d, pl.ds(c * HALF, HALF)]
            if t < ring.count[c][direction] and t + 1 != ring.jump:
                step(direction, t + 1, c).wait_recv()
                value = value + came[direction, t, c].astype(F32)
            sent[direction, t - 1, c] = value.astype(BF)
            step(direction, t, c).start()
        if number + 1 in aside:
            aside[number + 1]()
    make_term(0)
    halves = []
    for c in range(2):
        value = term[0, pl.ds(c * HALF, HALF)]
        for direction in range(2):
            for t in dict.fromkeys((1, ring.jump)):
                if t <= ring.count[c][direction]:
                    step(direction, t, c).wait_recv()
                    value = value + came[direction, t - 1, c].astype(F32)
        halves.append(value)
    for t in range(1, zs // 2 + 1):
        for direction, c in ring.each(t):
            step(direction, t, c).wait_send()
    whole = own.at[pl.ds(0, zs * slot)]
    for k in range(3):
        remote(whole, whole, peer_send.at[k], peer_recv.at[0, k], peers[k]).wait_send()
    return jnp.concatenate(halves, axis=0)


def main_kernel(zs, xs, slot, width, names, *refs):
    n = dict(zip(names, refs))
    place = Place(zs, xs)
    touch = 2 * zs * slot
    edges = n["heads"].shape[1]
    nrel = n["rel_table"].shape[1]
    seg = zs * RELS

    table_copy = pltpu.make_async_copy(n["relations"], n["rel_table"], n["table_sem"])
    table_copy.start()
    barrier = pltpu.get_barrier_semaphore()
    everyone = place.everyone()
    for device in everyone:
        pl.semaphore_signal(barrier, inc=1, device_id=device, device_id_type=MESH)
    emb, rel_vec = n["emb"], n["rel_vec"]
    emb[...] = jnp.zeros_like(emb)
    rel_vec[...] = jnp.zeros_like(rel_vec)
    emb[:, :width] = n["emb_in"][...]
    n["accum"][...] = column(n["accum_in"][...], PER)
    lane = iota((PER, 128), 1)

    def write_block(r):
        value = emb[...]
        block = n["block"].at[r]
        block[:, :TAIL] = value[:, :TAIL].astype(BF)
        block[:, TAIL:] = jnp.where(lane < width - TAIL, value[:, TAIL:], 0.0).astype(BF)
        requests = n["requests"][r].astype(BF)
        kj, q = requests.shape
        wanted = jnp.zeros((16, 128), F32)
        for yh in range(2):
            mine = iota((16, q), 0)
            pick = ((iota((16, q), 1) == mine + yh * zs) & (mine < zs)).astype(BF)
            put = (iota((kj, 128), 1) == iota((kj, 128), 0) + (MARK + yh * kj)).astype(BF)
            wanted = wanted + mm(mm(pick, requests, 1, 1).astype(BF), put, 1, 0)
        block[:16, TAIL:] = jnp.where(lane[:16] < width - TAIL, value[:16, TAIL:], wanted).astype(BF)

    write_block(0)

    def counts(ids):
        neg = ids.shape[1]
        hot = (iota((touch, neg), 0) == ids).astype(BF)
        return mm(jnp.ones((8, neg), BF), hot, 1, 1)[:1] * (1.0 / neg)

    def rel_column(r):
        return column(n["rel_ids"][r : r + 1, :], edges)

    for r in range(2):
        for side, name in enumerate(("own_neg", "far_neg")):
            n["count"][2 * r + side : 2 * r + side + 1, :] = counts(n[name][r : r + 1, :])
    table_copy.wait()
    for r in range(2):
        hot = (iota((edges, nrel), 1) == rel_column(r)).astype(BF)
        rel_vec[r, :, :width] = mm(hot, n["rel_table"][...], 1, 1)
    pl.semaphore_wait(barrier, len(everyone))

    def edge_step(r):
        own, far = n["own"][r], n["far"][r]
        head_hot = (iota((touch, edges), 0) == n["heads"][r : r + 1, :]).astype(BF)
        tail_hot = (iota((touch, edges), 0) == n["tails"][r : r + 1, :]).astype(BF)
        rel = rel_vec[r]
        head_vec = mm(head_hot, own, 0, 0)
        tail_vec = mm(tail_hot, far, 0, 0)
        positive = jnp.sum(head_vec * rel * tail_vec, axis=-1, keepdims=True)
        query_tail = (head_vec * rel).astype(BF)
        query_head = (tail_vec * rel).astype(BF)
        own_count = n["count"][2 * r : 2 * r + 1, :]
        far_count = n["count"][2 * r + 1 : 2 * r + 2, :]
        weight_tail = (jax.nn.sigmoid(mm(query_tail, far, 1, 1)) * far_count).astype(BF)
        weight_head = (jax.nn.sigmoid(mm(query_head, own, 1, 1)) * own_count).astype(BF)
        back_tail = mm(weight_tail, far, 1, 0)
        back_head = mm(weight_head, own, 1, 0)
        coeff = -jax.nn.sigmoid(-positive)

        def spread(hot, grad, weight, query):
            hi = grad.astype(BF)
            lo = (grad - hi.astype(F32)).astype(BF)
            return (mm(hot, hi, 1, 0) + mm(hot, lo, 1, 0) + mm(weight, query, 0, 0)).astype(BF)

        n["own_grad"][r] = spread(head_hot, rel * (coeff * tail_vec + back_tail), weight_head, query_head)
        n["far_grad"][r] = spread(tail_hot, rel * (coeff * head_vec + back_head), weight_tail, query_tail)
        grad_rel = coeff * head_vec * tail_vec + head_vec * back_tail + tail_vec * back_head
        rows = n["rows"].at[r, 0, pl.ds(0, edges)]
        rows[:, :TAIL] = grad_rel[:, :TAIL].astype(BF)
        at, ids = iota((edges, 128), 1), rel_column(r)
        marks = jnp.where(at == MARK, ids >> 6, jnp.where(at == MARK + 1, ids & 63, 0)).astype(F32)
        rows[:, TAIL:] = jnp.where(at < width - TAIL, grad_rel[:, TAIL:], marks).astype(BF)

    def update(row_grad):
        accum = n["accum"][...] + jnp.sum(row_grad * row_grad, axis=-1, keepdims=True) * (1.0 / width)
        n["accum"][...] = accum
        emb[...] = emb[...] - LEARN_RATE * row_grad / jnp.sqrt(accum)

    def slot_rows(r, near, d):
        return n["rows"].at[r, near, pl.ds(d * edges, edges)]

    def x_copy(r, e):
        return remote(slot_rows(r, 0, 0), slot_rows(r, 0, e), n["x_send"].at[r, e], n["x_recv"].at[r, e], place.along_x(xs - e))

    def core_copy(r, d):
        return remote(slot_rows(r, 0, d), slot_rows(r, 1, d), n["core_send"].at[r, d], n["core_recv"].at[r, d], (place.mate, place.s))

    def rows_start(r):
        for e in range(1, xs):
            x_copy(r, e).start()
        core_copy(r, 0).start()

    def rows_forward(r):
        for e in range(1, xs):
            x_copy(r, e).wait_recv()
            core_copy(r, e).start()

    def rows_sum(r):
        for d in range(xs):
            core_copy(r, d).wait_recv()
        base = (place.x * INNER + place.core) * (2 * seg)
        total = n["dense"][...] if r else jnp.zeros((4 * seg, WIDE), F32)
        for near in range(2):
            block = n["rows"][r, near]
            marks = block[:, TAIL:].astype(F32)
            at = iota(marks.shape, 1)
            ids = jnp.sum(jnp.where(at == MARK, marks * 64.0, jnp.where(at == MARK + 1, marks, 0.0)), axis=1, keepdims=True)
            col = iota((xs * edges, 4 * seg), 1)
            target = base + col + jnp.where(col >= 2 * seg, 2 * seg, 0)
            total = total + mm((ids.astype(I32) == target).astype(BF), block, 0, 0)
        n["dense"][...] = total
        for e in range(1, xs):
            x_copy(r, e).wait_send()
        for d in range(xs):
            core_copy(r, d).wait_send()

    def seg_rows(ylo, yh):
        return pl.ds(pl.multiple_of((ylo * 2 + yh) * seg, seg), seg)

    def y_copy(k):
        ylo = place.ylo if k == 0 else 1 - place.ylo
        yh = place.yh if k == 1 else 1 - place.yh
        return remote(n["y_out"].at[seg_rows(ylo, yh)], n["y_in"].at[k], n["y_send"].at[k], n["y_recv"].at[k], place.peers(1)[k])

    def y_start():
        n["y_out"][...] = n["dense"][...].astype(BF)
        for k in range(3):
            y_copy(k).start()

    def z_copy(e):
        src = n["z_out"].at[lax.rem(place.z + zs - e, zs)]
        return remote(src, n["z_in"].at[e], n["z_send"].at[e], n["z_recv"].at[e], place.along_z(zs - e))

    def z_start():
        total = n["dense"][seg_rows(place.ylo, place.yh), :]
        for k in range(3):
            y_copy(k).wait_recv()
            total = total + n["y_in"][k].astype(F32)
        total = total.astype(BF)
        row, col = iota((zs * 16, seg), 0), iota((zs * 16, seg), 1)
        zz, k = row >> 4, row & 15
        packed = jnp.zeros((zs * 16, 128), F32)
        full = TAIL // 128
        for c in range(full):
            j = k - c * RELS
            hot = ((col == zz * RELS + j) & (j >= 0) & (j < RELS)).astype(BF)
            packed = packed + mm(hot, total[:, c * 128 : (c + 1) * 128], 1, 0)
        rest = width - TAIL
        last = total[:, TAIL:].astype(F32)
        last = jnp.where(iota(last.shape, 1) < rest, last, 0.0)
        for j in range(RELS):
            hot = ((col == zz * RELS + j) & (k == full * RELS)).astype(BF)
            moved = last if j == 0 else pltpu.roll(last, j * rest, 1)
            packed = packed + mm(hot, moved.astype(BF), 1, 0)
        packed = packed.astype(BF)
        for zz in range(zs):
            n["z_out"][zz] = packed[zz * 16 : (zz + 1) * 16]
        for e in range(1, zs):
            z_copy(e).start()

    def z_end():
        total = n["z_out"][place.z].astype(F32)
        for e in range(1, zs):
            z_copy(e).wait_recv()
            total = total + n["z_in"][e].astype(F32)
        share = n["share"]
        share[...] = jnp.zeros_like(share)
        full, rest = TAIL // 128, width - TAIL
        for c in range(full):
            share[:RELS, c * 128 : (c + 1) * 128] = total[c * RELS : (c + 1) * RELS, :]
        for j in range(RELS):
            last = total[full * RELS : full * RELS + 1, :]
            last = last if j == 0 else pltpu.roll(last, 128 - j * rest, 1)
            share[j : j + 1, TAIL:] = jnp.where(iota((1, 128), 1) < rest, last, 0.0)
        value = share[...]
        squares = jnp.sum(value * value, axis=-1, keepdims=True) * (1.0 / width)
        rel_accum = column(n["rel_accum"][...], value.shape[0]) + squares
        rel_accum = jnp.where(iota(rel_accum.shape, 0) < RELS, rel_accum, 1.0)
        value = -LEARN_RATE * value / jnp.sqrt(rel_accum)
        n["step_out"][...] = value[:RELS, :width]
        n["rel_accum_out"][...] = as_row(rel_accum, RELS)
        for k in range(3):
            y_copy(k).wait_send()
        for e in range(1, zs):
            z_copy(e).wait_send()

    last_step = zs // 2
    for r in range(2):
        if r:
            write_block(r)
        fetch(
            place, r, slot, n["block"].at[r], n["line"].at[r], n["picked"].at[r], n["own"].at[r], n["far"].at[r], n["idx"].at[r],
            Ring(place, n["f_send"].at[r], n["f_recv"].at[r]), n["fp_send"].at[r], n["fp_recv"].at[r], n["f_self"].at[r],
        )
        edge_step(r)
        steps = {0: [functools.partial(rows_start, r)]}
        plan = ((2, functools.partial(rows_forward, r)), (4, functools.partial(rows_sum, r)))
        if r:
            plan = plan + ((4, y_start), (6, z_start))
        for t, what in plan:
            steps.setdefault(min(t, last_step), []).append(what)
        aside = {t: (lambda todo=todo: [f() for f in todo]) for t, todo in steps.items()}
        row_grad = give_back(
            place, r, slot, n["own_grad"].at[r], n["far_grad"].at[r], n["idx"].at[r], n["got"].at[r], n["term"], n["sent"].at[r], n["came"].at[r],
            Ring(place, n["s_send"].at[r], n["s_recv"].at[r]), n["sp_send"].at[r], n["sp_recv"].at[r], n["s_self"].at[r], aside,
        )
        update(row_grad)
    n["emb_out"][...] = emb[:, :width]
    n["accum_out"][...] = as_row(n["accum"][...], PER)
    z_end()


def run(inputs, zs, xs, slot):
    width = inputs["emb_in"].shape[1]
    touch = 2 * zs * slot
    edges = inputs["heads"].shape[1]
    half = zs // 2
    seg = zs * RELS
    dma = pltpu.SemaphoreType.DMA
    vmem = pltpu.VMEM
    outputs = dict(
        emb_out=jax.ShapeDtypeStruct((PER, width), F32),
        accum_out=jax.ShapeDtypeStruct((1, PER), F32),
        step_out=jax.ShapeDtypeStruct((RELS, width), F32),
        rel_accum_out=jax.ShapeDtypeStruct((1, RELS), F32),
    )
    scratch = dict(
        emb=vmem((PER, WIDE), F32),
        rel_table=vmem(inputs["relations"].shape, BF),
        accum=vmem((PER, 1), F32),
        share=vmem((8, WIDE), F32),
        rel_vec=vmem((2, edges, WIDE), F32),
        count=vmem((4, touch), F32),
        block=vmem((2, PER, WIDE), BF),
        line=vmem((2, zs, PER, WIDE), BF),
        picked=vmem((2, zs, PER, WIDE), BF),
        own=vmem((2, touch, WIDE), BF),
        far=vmem((2, touch, WIDE), BF),
        idx=vmem((2, zs, 128), F32),
        own_grad=vmem((2, touch, WIDE), BF),
        far_grad=vmem((2, touch, WIDE), BF),
        got=vmem((2, zs, PER, WIDE), BF),
        term=vmem((zs, PER, WIDE), F32),
        sent=vmem((2, 2, half, 2, HALF, WIDE), BF),
        came=vmem((2, 2, half, 2, HALF, WIDE), BF),
        rows=vmem((2, 2, xs * edges, WIDE), BF),
        dense=vmem((4 * seg, WIDE), F32),
        y_out=vmem((4 * seg, WIDE), BF),
        y_in=vmem((3, seg, WIDE), BF),
        z_out=vmem((zs, 16, 128), BF),
        z_in=vmem((zs, 16, 128), BF),
        table_sem=dma,
        f_send=dma((2, 2, half, 2)),
        f_recv=dma((2, 2, half, 2)),
        fp_send=dma((2, 3)),
        fp_recv=dma((2, 3)),
        f_self=dma((2,)),
        s_send=dma((2, 2, half, 2)),
        s_recv=dma((2, 2, half, 2)),
        sp_send=dma((2, 3)),
        sp_recv=dma((2, zs, 3)),
        s_self=dma((2, zs)),
        x_send=dma((2, xs)),
        x_recv=dma((2, xs)),
        core_send=dma((2, xs)),
        core_recv=dma((2, xs)),
        y_send=dma((3,)),
        y_recv=dma((3,)),
        z_send=dma((zs,)),
        z_recv=dma((zs,)),
    )
    in_vmem = pl.BlockSpec(memory_space=pltpu.VMEM)
    names = (*inputs, *outputs, *scratch)
    return pl.pallas_call(
        functools.partial(main_kernel, zs, xs, slot, width, names),
        name="train_step",
        out_shape=tuple(outputs.values()),
        in_specs=[pl.BlockSpec(memory_space=pl.ANY) if k == "relations" else in_vmem for k in inputs],
        out_specs=(in_vmem,) * len(outputs),
        scratch_shapes=list(scratch.values()),
        compiler_params=pltpu.CompilerParams(collective_id=0, has_side_effects=True),
    )(*inputs.values())


def body(embeddings, row_accum, relations, relation_accum, request_rows, head_slots, tail_slots, relation_ids, own_negatives, far_negatives):
    rounds, shards, sides, slot = request_rows.shape
    inputs = dict(
        emb_in=embeddings,
        accum_in=row_accum[None, :],
        relations=relations.T,
        rel_accum=relation_accum[None, :],
        requests=request_rows.transpose(0, 2, 3, 1).reshape(rounds, sides * slot, shards),
        heads=head_slots,
        tails=tail_slots,
        rel_ids=relation_ids,
        own_neg=own_negatives,
        far_neg=far_negatives,
    )
    emb, accum, step, rel_accum = run(inputs, shards // 2, lax.axis_size("dom") // INNER, slot)
    return (emb, accum[0], step, rel_accum[0])


def solution(mesh):
    both = ("dom", "shard")
    return jax.shard_map(
        body,
        mesh=mesh,
        in_specs=(P(both, None), P(both), P(), P(both), P(None, both, None, None)) + (P(None, both),) * 5,
        out_specs=(P(both, None), P(both), P(both, None), P(both)),
        check_vma=False,
    )
```

```python
import functools

import jax
import jax.numpy as jnp
from jax import lax
from jax.experimental import pallas as pl
from jax.experimental.pallas import tpu as pltpu
from jax.sharding import PartitionSpec as P

LEARN_RATE = 0.1
BF = jnp.bfloat16
F32 = jnp.float32
I32 = jnp.int32
MESH = pl.DeviceIdType.MESH
WIDE = 512
TAIL = WIDE - 128
MARK = 64
PER = 64
REST = 16
FULL = 3 * PER
PACKED = FULL + 16
CUTS = ((0, 112), (112, PACKED))
RELS = 5
INNER = 4


def mm(a, b, ca, cb):
    return lax.dot_general(a, b, (((ca,), (cb,)), ((), ())), preferred_element_type=F32)


def iota(shape, dim):
    return lax.broadcasted_iota(I32, shape, dim)


def hops(zs):
    return ((zs // 2, zs - 1 - zs // 2), (zs - 1 - zs // 2, zs // 2))


def column(row, rows):
    n = row.shape[1]
    return jnp.sum(jnp.where(iota((rows, n), 0) == iota((rows, n), 1), row, jnp.zeros_like(row)), axis=1, keepdims=True)


def as_row(col, n):
    rows = col.shape[0]
    return jnp.sum(jnp.where(iota((rows, n), 0) == iota((rows, n), 1), col, jnp.zeros_like(col)), axis=0, keepdims=True)


def remote(src, dst, send, recv, device):
    return pltpu.make_async_remote_copy(
        src_ref=src, dst_ref=dst, send_sem=send, recv_sem=recv, device_id=device, device_id_type=MESH
    )


class Place:
    def __init__(self, zs, xs):
        self.zs, self.xs = zs, xs
        g = lax.axis_index("dom")
        s = lax.axis_index("shard")
        self.g, self.s = g, s
        self.z = lax.rem(s, zs)
        self.yh = s // zs
        self.other = (1 - self.yh) * zs + self.z
        self.x = g // INNER
        self.inner = lax.rem(g, INNER)
        self.core = lax.rem(g, 2)
        self.ylo = self.inner // 2
        self.mate = g + 1 - 2 * self.core
        self.far_y = g + 2 - 4 * self.ylo

    def along_z(self, d):
        return (self.g, self.yh * self.zs + lax.rem(self.z + d, self.zs))

    def along_x(self, d):
        return (lax.rem(self.x + d, self.xs) * INNER + self.inner, self.s)

    def peers(self, r):
        h = self.mate if r == 0 else self.far_y
        return ((self.g, self.other), (h, self.s), (h, self.other))

    def everyone(self):
        return (
            [self.along_z(d) for d in range(1, self.zs)]
            + [self.along_x(d) for d in range(1, self.xs)]
            + list(self.peers(0))
            + list(self.peers(1)[1:])
        )

    def owner_rows(self, yh, d, slot):
        owner = yh * self.zs + lax.rem(self.z + d, self.zs)
        return pl.ds(pl.multiple_of(owner * slot, slot), slot)


class Ring:
    def __init__(self, place, send, recv):
        self.place, self.send, self.recv = place, send, recv
        self.count = hops(place.zs)
        self.far = place.zs // 2
        self.jump = place.zs // 4 + 1
        near, rest = list(range(1, self.jump)), list(range(self.jump, self.far + 1))
        self.order = []
        while near or rest:
            for lane in (near, rest):
                if lane:
                    self.order.append(lane.pop(0))

    def copy(self, src, dst, direction, t, c, hop):
        return remote(
            src, dst, self.send.at[direction, t - 1, c], self.recv.at[direction, t - 1, c],
            self.place.along_z(hop if direction == 0 else self.place.zs - hop),
        )

    def each(self, t):
        for c in range(2):
            for direction in range(2):
                if t <= self.count[c][direction]:
                    yield direction, c


def piece(ref, c):
    return ref.at[pl.ds(CUTS[c][0], CUTS[c][1] - CUTS[c][0])]


def fold(last):
    keep = iota((8, 128), 1) < REST
    total = jnp.zeros((8, 128), F32)
    for m in range(8):
        part = jnp.where(keep, last[m * 8 : (m + 1) * 8], 0.0)
        total = total + (part if m == 0 else pltpu.roll(part, m * REST, 1))
    return total


def unfold(folded):
    keep = iota((8, 128), 1) < REST
    parts = [folded if m == 0 else pltpu.roll(folded, 128 - m * REST, 1) for m in range(8)]
    return jnp.concatenate([jnp.where(keep, part, 0.0) for part in parts], axis=0)


def widen(packed, last):
    return jnp.concatenate([packed[c * PER : (c + 1) * PER] for c in range(3)] + [last], axis=1)


def fetch(place, r, slot, block, line, picked, own, far, idx, ring, peer_send, peer_recv, self_sem, beside):
    zs, peers = place.zs, place.peers(r)

    def step(direction, t, c):
        sign = -1 if direction == 0 else 1
        first = t in (1, ring.jump)
        src = piece(block, c) if first else piece(line.at[(sign * (t - 1)) % zs], c)
        return ring.copy(src, piece(line.at[(sign * t) % zs], c), direction, t, c, t if first else 1)

    def select(d):
        value = block[...] if d == 0 else line[d]
        tail = value[FULL:].astype(F32)
        table = tail[8:]
        ids = jnp.sum(jnp.where(iota(table.shape, 0) == lax.rem(place.z, 8), table, 0.0), axis=0, keepdims=True)
        ids = jnp.where(place.z >= 8, pltpu.roll(ids, 64, 1), ids)
        idx[d : d + 1, :] = ids
        hot = (iota((PER, PER), 0) == ids[:, :PER].astype(I32)).astype(BF)
        picked[d] = mm(hot, widen(value, unfold(tail[:8]).astype(BF)), 0, 0).astype(BF)
        at = place.owner_rows(place.yh, d, slot)
        mine = place.yh * 2 * slot
        theirs = (1 - place.yh) * 2 * slot
        pltpu.make_async_copy(picked.at[d, pl.ds(mine, slot)], own.at[at], self_sem).start()
        for k, (start, dst) in enumerate(((theirs, own), (mine + slot, far), (theirs + slot, far))):
            remote(picked.at[d, pl.ds(start, slot)], dst.at[at], peer_send.at[k], peer_recv.at[k], peers[k]).start()

    for t in dict.fromkeys((ring.jump, 1)):
        for direction, c in ring.each(t):
            step(direction, t, c).start()
    select(0)
    beside()
    for t in ring.order:
        for direction, c in ring.each(t):
            step(direction, t, c).wait_recv()
            if t + 1 <= ring.count[c][direction] and t + 1 != ring.jump:
                step(direction, t + 1, c).start()
        select(zs - t)
        if t != zs // 2:
            select(t)
    for t in range(1, zs // 2 + 1):
        for direction, c in ring.each(t):
            step(direction, t, c).wait_send()
    whole = own.at[pl.ds(0, zs * slot)]
    pltpu.make_async_copy(whole, whole, self_sem).wait()
    for k in range(3):
        copy = remote(whole, whole, peer_send.at[k], peer_recv.at[k], peers[k])
        copy.wait_send()
        copy.wait_recv()


def give_back(place, r, slot, own, far, idx, got, term, sent, came, ring, peer_send, peer_recv, self_sem, aside):
    zs, peers = place.zs, place.peers(r)
    mine = place.yh * 2 * slot

    def exchange(d):
        here, there = place.owner_rows(place.yh, d, slot), place.owner_rows(1 - place.yh, d, slot)
        k0, k1 = got.at[d, pl.ds(mine, slot)], got.at[d, pl.ds(mine + slot, slot)]
        return (
            pltpu.make_async_copy(own.at[here], k0, self_sem.at[d]),
            remote(own.at[there], k0, peer_send.at[0], peer_recv.at[d, 0], peers[0]),
            remote(far.at[here], k1, peer_send.at[1], peer_recv.at[d, 1], peers[1]),
            remote(far.at[there], k1, peer_send.at[2], peer_recv.at[d, 2], peers[2]),
        )

    def step(direction, d, c):
        hop = d if d == ring.jump else 1
        return ring.copy(piece(sent.at[direction, d - 1], c), piece(came.at[direction, d - 1], c), direction, d, c, hop)

    def make_term(d):
        copies = exchange(d)
        copies[0].wait()
        for copy in copies[1:]:
            copy.wait_recv()
        hot = (iota((PER, PER), 0) == idx[d : d + 1, :PER].astype(I32)).astype(BF)
        value = mm(hot, got[d], 1, 0)
        for c in range(3):
            term[d, c * PER : (c + 1) * PER] = value[:, c * 128 : (c + 1) * 128]
        term[d, FULL:] = jnp.concatenate([fold(value[:, TAIL:]), jnp.zeros((8, 128), F32)], axis=0)

    order = ring.order[::-1]
    order = sorted(order, key=lambda t: (ring.far - t) if t >= ring.jump else (ring.jump - 1 - t) + 1.5)
    for t in order:
        for d in (t,) if t == ring.far else (t, zs - t):
            for copy in exchange(d):
                copy.start()
    for copy in exchange(0):
        copy.start()
    aside[0]()
    made = set()
    for number, t in enumerate(order):
        for direction, c in ring.each(t):
            d = t if direction == 0 else zs - t
            if d not in made:
                make_term(d)
                made.add(d)
            low, high = CUTS[c]
            value = term[d, low:high]
            if t < ring.count[c][direction] and t + 1 != ring.jump:
                step(direction, t + 1, c).wait_recv()
                value = value + came[direction, t, low:high].astype(F32)
            sent[direction, t - 1, low:high] = value.astype(BF)
            step(direction, t, c).start()
        if number + 1 in aside:
            aside[number + 1]()
    make_term(0)
    halves = []
    for c in range(2):
        low, high = CUTS[c]
        value = term[0, low:high]
        for direction in range(2):
            for t in dict.fromkeys((1, ring.jump)):
                if t <= ring.count[c][direction]:
                    step(direction, t, c).wait_recv()
                    value = value + came[direction, t - 1, low:high].astype(F32)
        halves.append(value)
    for t in range(1, zs // 2 + 1):
        for direction, c in ring.each(t):
            step(direction, t, c).wait_send()
    whole = own.at[pl.ds(0, zs * slot)]
    for k in range(3):
        remote(whole, whole, peer_send.at[k], peer_recv.at[0, k], peers[k]).wait_send()
    total = jnp.concatenate(halves, axis=0)
    return widen(total, unfold(total[FULL : FULL + 8]))


def main_kernel(zs, xs, slot, width, names, *refs):
    n = dict(zip(names, refs))
    place = Place(zs, xs)
    touch = 2 * zs * slot
    edges = n["heads"].shape[1]
    nrel = n["rel_table"].shape[1]
    seg = zs * RELS

    table_copy = pltpu.make_async_copy(n["relations"], n["rel_table"], n["table_sem"])
    table_copy.start()
    barrier = pltpu.get_barrier_semaphore()
    everyone = place.everyone()
    for device in everyone:
        pl.semaphore_signal(barrier, inc=1, device_id=device, device_id_type=MESH)
    emb, rel_vec = n["emb"], n["rel_vec"]
    emb[...] = jnp.zeros_like(emb)
    rel_vec[...] = jnp.zeros_like(rel_vec)
    emb[:, :width] = n["emb_in"][...]
    n["accum"][...] = column(n["accum_in"][...], PER)

    def write_block(r):
        value = emb[...]
        block = n["block"].at[r]
        for c in range(3):
            block[c * PER : (c + 1) * PER] = value[:, c * 128 : (c + 1) * 128].astype(BF)
        requests = n["requests"][r].astype(BF)
        kj, q = requests.shape
        wanted = jnp.zeros((8, 128), F32)
        for part in range(2):
            for yh in range(2):
                at = iota((8, q), 0) + part * 8
                pick = ((iota((8, q), 1) == at + yh * zs) & (at < zs)).astype(BF)
                put = (iota((kj, 128), 1) == iota((kj, 128), 0) + (part * 64 + yh * kj)).astype(BF)
                wanted = wanted + mm(mm(pick, requests, 1, 1).astype(BF), put, 1, 0)
        block[FULL:] = jnp.concatenate([fold(value[:, TAIL:]), wanted], axis=0).astype(BF)

    write_block(0)

    def counts(ids):
        neg = ids.shape[1]
        hot = (iota((touch, neg), 0) == ids).astype(BF)
        return mm(jnp.ones((8, neg), BF), hot, 1, 1)[:1] * (1.0 / neg)

    def rel_column(r):
        return column(n["rel_ids"][r : r + 1, :], edges)

    for r in range(2):
        for side, name in enumerate(("own_neg", "far_neg")):
            n["count"][2 * r + side : 2 * r + side + 1, :] = counts(n[name][r : r + 1, :])
    table_copy.wait()
    for r in range(2):
        hot = (iota((edges, nrel), 1) == rel_column(r)).astype(BF)
        rel_vec[r, :, :width] = mm(hot, n["rel_table"][...], 1, 1)
    pl.semaphore_wait(barrier, len(everyone))

    def edge_step(r):
        own, far = n["own"][r], n["far"][r]
        head_hot = (iota((touch, edges), 0) == n["heads"][r : r + 1, :]).astype(BF)
        tail_hot = (iota((touch, edges), 0) == n["tails"][r : r + 1, :]).astype(BF)
        rel = rel_vec[r]
        head_vec = mm(head_hot, own, 0, 0)
        tail_vec = mm(tail_hot, far, 0, 0)
        positive = jnp.sum(head_vec * rel * tail_vec, axis=-1, keepdims=True)
        query_tail = (head_vec * rel).astype(BF)
        query_head = (tail_vec * rel).astype(BF)
        own_count = n["count"][2 * r : 2 * r + 1, :]
        far_count = n["count"][2 * r + 1 : 2 * r + 2, :]
        weight_tail = (jax.nn.sigmoid(mm(query_tail, far, 1, 1)) * far_count).astype(BF)
        weight_head = (jax.nn.sigmoid(mm(query_head, own, 1, 1)) * own_count).astype(BF)
        back_tail = mm(weight_tail, far, 1, 0)
        back_head = mm(weight_head, own, 1, 0)
        coeff = -jax.nn.sigmoid(-positive)

        def spread(hot, grad, weight, query):
            hi = grad.astype(BF)
            lo = (grad - hi.astype(F32)).astype(BF)
            return (mm(hot, hi, 1, 0) + mm(hot, lo, 1, 0) + mm(weight, query, 0, 0)).astype(BF)

        n["own_grad"][r] = spread(head_hot, rel * (coeff * tail_vec + back_tail), weight_head, query_head)
        n["far_grad"][r] = spread(tail_hot, rel * (coeff * head_vec + back_head), weight_tail, query_tail)
        grad_rel = coeff * head_vec * tail_vec + head_vec * back_tail + tail_vec * back_head
        rows = n["rows"].at[r, 0, pl.ds(0, edges)]
        rows[:, :TAIL] = grad_rel[:, :TAIL].astype(BF)
        at, ids = iota((edges, 128), 1), rel_column(r)
        marks = jnp.where(at == MARK, ids >> 6, jnp.where(at == MARK + 1, ids & 63, 0)).astype(F32)
        rows[:, TAIL:] = jnp.where(at < width - TAIL, grad_rel[:, TAIL:], marks).astype(BF)

    def update(row_grad):
        accum = n["accum"][...] + jnp.sum(row_grad * row_grad, axis=-1, keepdims=True) * (1.0 / width)
        n["accum"][...] = accum
        emb[...] = emb[...] - LEARN_RATE * row_grad / jnp.sqrt(accum)

    def slot_rows(r, near, d):
        return n["rows"].at[r, near, pl.ds(d * edges, edges)]

    def x_copy(r, e):
        return remote(slot_rows(r, 0, 0), slot_rows(r, 0, e), n["x_send"].at[r, e], n["x_recv"].at[r, e], place.along_x(xs - e))

    def core_copy(r, d):
        return remote(slot_rows(r, 0, d), slot_rows(r, 1, d), n["core_send"].at[r, d], n["core_recv"].at[r, d], (place.mate, place.s))

    def rows_start(r):
        for e in range(1, xs):
            x_copy(r, e).start()
        core_copy(r, 0).start()

    def rows_forward(r):
        for e in range(1, xs):
            x_copy(r, e).wait_recv()
            core_copy(r, e).start()

    def rows_sum(r):
        for d in range(xs):
            core_copy(r, d).wait_recv()
        base = (place.x * INNER + place.core) * (2 * seg)
        total = n["dense"][...] if r else jnp.zeros((4 * seg, WIDE), F32)
        for near in range(2):
            block = n["rows"][r, near]
            marks = block[:, TAIL:].astype(F32)
            at = iota(marks.shape, 1)
            ids = jnp.sum(jnp.where(at == MARK, marks * 64.0, jnp.where(at == MARK + 1, marks, 0.0)), axis=1, keepdims=True)
            col = iota((xs * edges, 4 * seg), 1)
            target = base + col + jnp.where(col >= 2 * seg, 2 * seg, 0)
            total = total + mm((ids.astype(I32) == target).astype(BF), block, 0, 0)
        n["dense"][...] = total
        for e in range(1, xs):
            x_copy(r, e).wait_send()
        for d in range(xs):
            core_copy(r, d).wait_send()

    def seg_rows(ylo, yh):
        return pl.ds(pl.multiple_of((ylo * 2 + yh) * seg, seg), seg)

    def y_copy(k):
        ylo = place.ylo if k == 0 else 1 - place.ylo
        yh = place.yh if k == 1 else 1 - place.yh
        return remote(n["y_out"].at[seg_rows(ylo, yh)], n["y_in"].at[k], n["y_send"].at[k], n["y_recv"].at[k], place.peers(1)[k])

    def y_start():
        n["y_out"][...] = n["dense"][...].astype(BF)
        for k in range(3):
            y_copy(k).start()

    def z_copy(e):
        src = n["z_out"].at[lax.rem(place.z + zs - e, zs)]
        return remote(src, n["z_in"].at[e], n["z_send"].at[e], n["z_recv"].at[e], place.along_z(zs - e))

    def z_start():
        total = n["dense"][seg_rows(place.ylo, place.yh), :]
        for k in range(3):
            y_copy(k).wait_recv()
            total = total + n["y_in"][k].astype(F32)
        total = total.astype(BF)
        row, col = iota((zs * 16, seg), 0), iota((zs * 16, seg), 1)
        zz, k = row >> 4, row & 15
        packed = jnp.zeros((zs * 16, 128), F32)
        full = TAIL // 128
        for c in range(full):
            j = k - c * RELS
            hot = ((col == zz * RELS + j) & (j >= 0) & (j < RELS)).astype(BF)
            packed = packed + mm(hot, total[:, c * 128 : (c + 1) * 128], 1, 0)
        rest = width - TAIL
        last = total[:, TAIL:].astype(F32)
        last = jnp.where(iota(last.shape, 1) < rest, last, 0.0)
        for j in range(RELS):
            hot = ((col == zz * RELS + j) & (k == full * RELS)).astype(BF)
            moved = last if j == 0 else pltpu.roll(last, j * rest, 1)
            packed = packed + mm(hot, moved.astype(BF), 1, 0)
        packed = packed.astype(BF)
        for zz in range(zs):
            n["z_out"][zz] = packed[zz * 16 : (zz + 1) * 16]
        for e in range(1, zs):
            z_copy(e).start()

    def z_end():
        total = n["z_out"][place.z].astype(F32)
        for e in range(1, zs):
            z_copy(e).wait_recv()
            total = total + n["z_in"][e].astype(F32)
        share = n["share"]
        share[...] = jnp.zeros_like(share)
        full, rest = TAIL // 128, width - TAIL
        for c in range(full):
            share[:RELS, c * 128 : (c + 1) * 128] = total[c * RELS : (c + 1) * RELS, :]
        for j in range(RELS):
            last = total[full * RELS : full * RELS + 1, :]
            last = last if j == 0 else pltpu.roll(last, 128 - j * rest, 1)
            share[j : j + 1, TAIL:] = jnp.where(iota((1, 128), 1) < rest, last, 0.0)
        value = share[...]
        squares = jnp.sum(value * value, axis=-1, keepdims=True) * (1.0 / width)
        rel_accum = column(n["rel_accum"][...], value.shape[0]) + squares
        rel_accum = jnp.where(iota(rel_accum.shape, 0) < RELS, rel_accum, 1.0)
        value = -LEARN_RATE * value / jnp.sqrt(rel_accum)
        n["step_out"][...] = value[:RELS, :width]
        n["rel_accum_out"][...] = as_row(rel_accum, RELS)
        for k in range(3):
            y_copy(k).wait_send()
        for e in range(1, zs):
            z_copy(e).wait_send()

    last_step = zs // 2
    for r in range(2):
        if r:
            write_block(r)
        fetch(
            place, r, slot, n["block"].at[r], n["line"].at[r], n["picked"].at[r], n["own"].at[r], n["far"].at[r], n["idx"].at[r],
            Ring(place, n["f_send"].at[r], n["f_recv"].at[r]), n["fp_send"].at[r], n["fp_recv"].at[r], n["f_self"].at[r],
            functools.partial(rows_sum, 0) if r else (lambda: None),
        )
        edge_step(r)
        steps = {0: [functools.partial(rows_start, r)]}
        plan = ((2, functools.partial(rows_forward, r)),)
        if r:
            plan = plan + ((4, functools.partial(rows_sum, r)), (4, y_start), (6, z_start))
        for t, what in plan:
            steps.setdefault(min(t, last_step), []).append(what)
        aside = {t: (lambda todo=todo: [f() for f in todo]) for t, todo in steps.items()}
        row_grad = give_back(
            place, r, slot, n["own_grad"].at[r], n["far_grad"].at[r], n["idx"].at[r], n["got"].at[r], n["term"], n["sent"].at[r], n["came"].at[r],
            Ring(place, n["s_send"].at[r], n["s_recv"].at[r]), n["sp_send"].at[r], n["sp_recv"].at[r], n["s_self"].at[r], aside,
        )
        update(row_grad)
    n["emb_out"][...] = emb[:, :width]
    n["accum_out"][...] = as_row(n["accum"][...], PER)
    z_end()


def run(inputs, zs, xs, slot):
    width = inputs["emb_in"].shape[1]
    touch = 2 * zs * slot
    edges = inputs["heads"].shape[1]
    half = zs // 2
    seg = zs * RELS
    dma = pltpu.SemaphoreType.DMA
    vmem = pltpu.VMEM
    outputs = dict(
        emb_out=jax.ShapeDtypeStruct((PER, width), F32),
        accum_out=jax.ShapeDtypeStruct((1, PER), F32),
        step_out=jax.ShapeDtypeStruct((RELS, width), F32),
        rel_accum_out=jax.ShapeDtypeStruct((1, RELS), F32),
    )
    scratch = dict(
        emb=vmem((PER, WIDE), F32),
        rel_table=vmem(inputs["relations"].shape, BF),
        accum=vmem((PER, 1), F32),
        share=vmem((8, WIDE), F32),
        rel_vec=vmem((2, edges, WIDE), F32),
        count=vmem((4, touch), F32),
        block=vmem((2, PACKED, 128), BF),
        line=vmem((2, zs, PACKED, 128), BF),
        picked=vmem((2, zs, PER, WIDE), BF),
        own=vmem((2, touch, WIDE), BF),
        far=vmem((2, touch, WIDE), BF),
        idx=vmem((2, zs, 128), F32),
        own_grad=vmem((2, touch, WIDE), BF),
        far_grad=vmem((2, touch, WIDE), BF),
        got=vmem((2, zs, PER, WIDE), BF),
        term=vmem((zs, PACKED, 128), F32),
        sent=vmem((2, 2, half, PACKED, 128), BF),
        came=vmem((2, 2, half, PACKED, 128), BF),
        rows=vmem((2, 2, xs * edges, WIDE), BF),
        dense=vmem((4 * seg, WIDE), F32),
        y_out=vmem((4 * seg, WIDE), BF),
        y_in=vmem((3, seg, WIDE), BF),
        z_out=vmem((zs, 16, 128), BF),
        z_in=vmem((zs, 16, 128), BF),
        table_sem=dma,
        f_send=dma((2, 2, half, 2)),
        f_recv=dma((2, 2, half, 2)),
        fp_send=dma((2, 3)),
        fp_recv=dma((2, 3)),
        f_self=dma((2,)),
        s_send=dma((2, 2, half, 2)),
        s_recv=dma((2, 2, half, 2)),
        sp_send=dma((2, 3)),
        sp_recv=dma((2, zs, 3)),
        s_self=dma((2, zs)),
        x_send=dma((2, xs)),
        x_recv=dma((2, xs)),
        core_send=dma((2, xs)),
        core_recv=dma((2, xs)),
        y_send=dma((3,)),
        y_recv=dma((3,)),
        z_send=dma((zs,)),
        z_recv=dma((zs,)),
    )
    in_vmem = pl.BlockSpec(memory_space=pltpu.VMEM)
    names = (*inputs, *outputs, *scratch)
    return pl.pallas_call(
        functools.partial(main_kernel, zs, xs, slot, width, names),
        name="train_step",
        out_shape=tuple(outputs.values()),
        in_specs=[pl.BlockSpec(memory_space=pl.ANY) if k == "relations" else in_vmem for k in inputs],
        out_specs=(in_vmem,) * len(outputs),
        scratch_shapes=list(scratch.values()),
        compiler_params=pltpu.CompilerParams(collective_id=0, has_side_effects=True),
    )(*inputs.values())


def finish_kernel(*refs):
    half = len(refs) // 2
    for src, dst in zip(refs[:half], refs[half:]):
        dst[...] = src[...]


def finish(*values):
    in_vmem = pl.BlockSpec(memory_space=pltpu.VMEM)
    return pl.pallas_call(
        finish_kernel,
        name="finish",
        out_shape=tuple(jax.ShapeDtypeStruct(v.shape, v.dtype) for v in values),
        in_specs=[in_vmem] * len(values),
        out_specs=(in_vmem,) * len(values),
    )(*values)


def body(embeddings, row_accum, relations, relation_accum, request_rows, head_slots, tail_slots, relation_ids, own_negatives, far_negatives):
    rounds, shards, sides, slot = request_rows.shape
    inputs = dict(
        emb_in=embeddings,
        accum_in=row_accum[None, :],
        relations=relations.T,
        rel_accum=relation_accum[None, :],
        requests=request_rows.transpose(0, 2, 3, 1).reshape(rounds, sides * slot, shards),
        heads=head_slots,
        tails=tail_slots,
        rel_ids=relation_ids,
        own_neg=own_negatives,
        far_neg=far_negatives,
    )
    emb, accum, step, rel_accum = finish(*run(inputs, shards // 2, lax.axis_size("dom") // INNER, slot))
    return (emb, accum[0], step, rel_accum[0])


def solution(mesh):
    both = ("dom", "shard")
    return jax.shard_map(
        body,
        mesh=mesh,
        in_specs=(P(both, None), P(both), P(), P(both), P(None, both, None, None)) + (P(None, both),) * 5,
        out_specs=(P(both, None), P(both), P(both, None), P(both)),
        check_vma=False,
    )
```

```python
import functools

import jax
import jax.numpy as jnp
from jax import lax
from jax.experimental import pallas as pl
from jax.experimental.pallas import tpu as pltpu
from jax.sharding import PartitionSpec as P

LEARN_RATE = 0.1
BF = jnp.bfloat16
F32 = jnp.float32
I32 = jnp.int32
MESH = pl.DeviceIdType.MESH
WIDE = 512
TAIL = WIDE - 128
MARK = 64
PER = 64
REST = 16
FULL = 3 * PER
PACKED = FULL + 16
CUTS = ((0, 112), (112, PACKED))
RELS = 5
INNER = 4


def mm(a, b, ca, cb):
    return lax.dot_general(a, b, (((ca,), (cb,)), ((), ())), preferred_element_type=F32)


def iota(shape, dim):
    return lax.broadcasted_iota(I32, shape, dim)


def hops(zs):
    return ((zs // 2, zs - 1 - zs // 2), (zs - 1 - zs // 2, zs // 2))


def column(row, rows):
    n = row.shape[1]
    return jnp.sum(jnp.where(iota((rows, n), 0) == iota((rows, n), 1), row, jnp.zeros_like(row)), axis=1, keepdims=True)


def as_row(col, n):
    rows = col.shape[0]
    return jnp.sum(jnp.where(iota((rows, n), 0) == iota((rows, n), 1), col, jnp.zeros_like(col)), axis=0, keepdims=True)


def remote(src, dst, send, recv, device):
    return pltpu.make_async_remote_copy(
        src_ref=src, dst_ref=dst, send_sem=send, recv_sem=recv, device_id=device, device_id_type=MESH
    )


class Place:
    def __init__(self, zs, xs):
        self.zs, self.xs = zs, xs
        g = lax.axis_index("dom")
        s = lax.axis_index("shard")
        self.g, self.s = g, s
        self.z = lax.rem(s, zs)
        self.yh = s // zs
        self.other = (1 - self.yh) * zs + self.z
        self.x = g // INNER
        self.inner = lax.rem(g, INNER)
        self.core = lax.rem(g, 2)
        self.ylo = self.inner // 2
        self.mate = g + 1 - 2 * self.core
        self.far_y = g + 2 - 4 * self.ylo

    def along_z(self, d):
        return (self.g, self.yh * self.zs + lax.rem(self.z + d, self.zs))

    def along_x(self, d):
        return (lax.rem(self.x + d, self.xs) * INNER + self.inner, self.s)

    def peers(self, r):
        h = self.mate if r == 0 else self.far_y
        return ((self.g, self.other), (h, self.s), (h, self.other))

    def everyone(self):
        return (
            [self.along_z(d) for d in range(1, self.zs)]
            + [self.along_x(d) for d in range(1, self.xs)]
            + list(self.peers(0))
            + list(self.peers(1)[1:])
        )

    def owner_rows(self, yh, d, slot):
        owner = yh * self.zs + lax.rem(self.z + d, self.zs)
        return pl.ds(pl.multiple_of(owner * slot, slot), slot)


class Ring:
    def __init__(self, place, send, recv):
        self.place, self.send, self.recv = place, send, recv
        self.count = hops(place.zs)
        self.far = place.zs // 2
        self.jump = place.zs // 4 + 1
        self.order = sorted(range(1, self.far + 1), key=lambda t: 1.0 * t if t < self.jump else t - self.jump + 1.1)

    def copy(self, src, dst, direction, t, c, hop):
        return remote(
            src, dst, self.send.at[direction, t - 1, c], self.recv.at[direction, t - 1, c],
            self.place.along_z(hop if direction == 0 else self.place.zs - hop),
        )

    def each(self, t):
        for c in range(2):
            for direction in range(2):
                if t <= self.count[c][direction]:
                    yield direction, c


def piece(ref, c):
    return ref.at[pl.ds(CUTS[c][0], CUTS[c][1] - CUTS[c][0])]


def fold(last):
    keep = iota((8, 128), 1) < REST
    total = jnp.zeros((8, 128), F32)
    for m in range(8):
        part = jnp.where(keep, last[m * 8 : (m + 1) * 8], 0.0)
        total = total + (part if m == 0 else pltpu.roll(part, m * REST, 1))
    return total


def unfold(folded):
    keep = iota((8, 128), 1) < REST
    parts = [folded if m == 0 else pltpu.roll(folded, 128 - m * REST, 1) for m in range(8)]
    return jnp.concatenate([jnp.where(keep, part, 0.0) for part in parts], axis=0)


def widen(packed, last):
    return jnp.concatenate([packed[c * PER : (c + 1) * PER] for c in range(3)] + [last], axis=1)


def fetch(place, r, slot, block, line, picked, own, far, idx, ring, peer_send, peer_recv, self_sem, beside):
    zs, peers = place.zs, place.peers(r)

    def step(direction, t, c):
        sign = -1 if direction == 0 else 1
        first = t in (1, ring.jump)
        src = piece(block, c) if first else piece(line.at[(sign * (t - 1)) % zs], c)
        return ring.copy(src, piece(line.at[(sign * t) % zs], c), direction, t, c, t if first else 1)

    def select(d):
        value = block[...] if d == 0 else line[d]
        tail = value[FULL:].astype(F32)
        table = tail[8:]
        ids = jnp.sum(jnp.where(iota(table.shape, 0) == lax.rem(place.z, 8), table, 0.0), axis=0, keepdims=True)
        ids = jnp.where(place.z >= 8, pltpu.roll(ids, 64, 1), ids)
        idx[d : d + 1, :] = ids
        hot = (iota((PER, PER), 0) == ids[:, :PER].astype(I32)).astype(BF)
        picked[d] = mm(hot, widen(value, unfold(tail[:8]).astype(BF)), 0, 0).astype(BF)
        at = place.owner_rows(place.yh, d, slot)
        mine = place.yh * 2 * slot
        theirs = (1 - place.yh) * 2 * slot
        pltpu.make_async_copy(picked.at[d, pl.ds(mine, slot)], own.at[at], self_sem).start()
        for k, (start, dst) in enumerate(((theirs, own), (mine + slot, far), (theirs + slot, far))):
            remote(picked.at[d, pl.ds(start, slot)], dst.at[at], peer_send.at[k], peer_recv.at[k], peers[k]).start()

    for t in dict.fromkeys((ring.jump, 1)):
        for direction, c in ring.each(t):
            step(direction, t, c).start()
    select(0)
    for number, t in enumerate(ring.order):
        if number in beside:
            beside[number]()

        for direction, c in ring.each(t):
            step(direction, t, c).wait_recv()
            if t + 1 <= ring.count[c][direction] and t + 1 != ring.jump:
                step(direction, t + 1, c).start()
        select(zs - t)
        if t != zs // 2:
            select(t)
    for t in range(1, zs // 2 + 1):
        for direction, c in ring.each(t):
            step(direction, t, c).wait_send()
    whole = own.at[pl.ds(0, zs * slot)]
    pltpu.make_async_copy(whole, whole, self_sem).wait()
    for k in range(3):
        copy = remote(whole, whole, peer_send.at[k], peer_recv.at[k], peers[k])
        copy.wait_send()
        copy.wait_recv()


def give_back(place, r, slot, own, far, idx, got, term, sent, came, ring, peer_send, peer_recv, self_sem, aside):
    zs, peers = place.zs, place.peers(r)
    mine = place.yh * 2 * slot

    def exchange(d):
        here, there = place.owner_rows(place.yh, d, slot), place.owner_rows(1 - place.yh, d, slot)
        k0, k1 = got.at[d, pl.ds(mine, slot)], got.at[d, pl.ds(mine + slot, slot)]
        return (
            pltpu.make_async_copy(own.at[here], k0, self_sem.at[d]),
            remote(own.at[there], k0, peer_send.at[0], peer_recv.at[d, 0], peers[0]),
            remote(far.at[here], k1, peer_send.at[1], peer_recv.at[d, 1], peers[1]),
            remote(far.at[there], k1, peer_send.at[2], peer_recv.at[d, 2], peers[2]),
        )

    def step(direction, d, c):
        hop = d if d == ring.jump else 1
        return ring.copy(piece(sent.at[direction, d - 1], c), piece(came.at[direction, d - 1], c), direction, d, c, hop)

    def make_term(d):
        copies = exchange(d)
        copies[0].wait()
        for copy in copies[1:]:
            copy.wait_recv()
        hot = (iota((PER, PER), 0) == idx[d : d + 1, :PER].astype(I32)).astype(BF)
        value = mm(hot, got[d], 1, 0)
        for c in range(3):
            term[d, c * PER : (c + 1) * PER] = value[:, c * 128 : (c + 1) * 128]
        term[d, FULL:] = jnp.concatenate([fold(value[:, TAIL:]), jnp.zeros((8, 128), F32)], axis=0)

    order = sorted(range(1, ring.far + 1), key=lambda t: (ring.far - t) if t >= ring.jump else (ring.jump - 1 - t) + 1.5)
    for t in order:
        for d in (t,) if t == ring.far else (t, zs - t):
            for copy in exchange(d):
                copy.start()
    for copy in exchange(0):
        copy.start()
    aside[0]()
    made = set()

    def chained(t, direction, c):
        return t < ring.count[c][direction] and t + 1 != ring.jump

    def pass_on(t, direction, c):
        d = t if direction == 0 else zs - t
        if d not in made:
            make_term(d)
            made.add(d)
        low, high = CUTS[c]
        value = term[d, low:high]
        if chained(t, direction, c):
            step(direction, t + 1, c).wait_recv()
            value = value + came[direction, t, low:high].astype(F32)
        sent[direction, t - 1, low:high] = value.astype(BF)
        step(direction, t, c).start()

    for t in order:
        for direction, c in ring.each(t):
            if not chained(t, direction, c):
                pass_on(t, direction, c)
    for number, t in enumerate(order):
        for direction, c in ring.each(t):
            if chained(t, direction, c):
                pass_on(t, direction, c)
        if number + 1 in aside:
            aside[number + 1]()
    make_term(0)
    halves = []
    for c in range(2):
        low, high = CUTS[c]
        value = term[0, low:high]
        for direction in range(2):
            for t in dict.fromkeys((1, ring.jump)):
                if t <= ring.count[c][direction]:
                    step(direction, t, c).wait_recv()
                    value = value + came[direction, t - 1, low:high].astype(F32)
        halves.append(value)
    for t in range(1, zs // 2 + 1):
        for direction, c in ring.each(t):
            step(direction, t, c).wait_send()
    whole = own.at[pl.ds(0, zs * slot)]
    for k in range(3):
        remote(whole, whole, peer_send.at[k], peer_recv.at[0, k], peers[k]).wait_send()
    total = jnp.concatenate(halves, axis=0)
    return widen(total, unfold(total[FULL : FULL + 8]))


def main_kernel(zs, xs, slot, width, names, *refs):
    n = dict(zip(names, refs))
    place = Place(zs, xs)
    touch = 2 * zs * slot
    edges = n["heads"].shape[1]
    nrel = n["rel_table"].shape[1]
    seg = zs * RELS

    table_copy = pltpu.make_async_copy(n["relations"], n["rel_table"], n["table_sem"])
    table_copy.start()
    barrier = pltpu.get_barrier_semaphore()
    everyone = place.everyone()
    for device in everyone:
        pl.semaphore_signal(barrier, inc=1, device_id=device, device_id_type=MESH)
    emb, rel_vec = n["emb"], n["rel_vec"]
    emb[...] = jnp.zeros_like(emb)
    rel_vec[...] = jnp.zeros_like(rel_vec)
    emb[:, :width] = n["emb_in"][...]
    n["accum"][...] = column(n["accum_in"][...], PER)

    def write_block(r):
        value = emb[...]
        block = n["block"].at[r]
        for c in range(3):
            block[c * PER : (c + 1) * PER] = value[:, c * 128 : (c + 1) * 128].astype(BF)
        requests = n["requests"][r].astype(BF)
        kj, q = requests.shape
        wanted = jnp.zeros((8, 128), F32)
        for part in range(2):
            for yh in range(2):
                at = iota((8, q), 0) + part * 8
                pick = ((iota((8, q), 1) == at + yh * zs) & (at < zs)).astype(BF)
                put = (iota((kj, 128), 1) == iota((kj, 128), 0) + (part * 64 + yh * kj)).astype(BF)
                wanted = wanted + mm(mm(pick, requests, 1, 1).astype(BF), put, 1, 0)
        block[FULL:] = jnp.concatenate([fold(value[:, TAIL:]), wanted], axis=0).astype(BF)

    write_block(0)

    def counts(ids):
        neg = ids.shape[1]
        hot = (iota((touch, neg), 0) == ids).astype(BF)
        return mm(jnp.ones((8, neg), BF), hot, 1, 1)[:1] * (1.0 / neg)

    def rel_column(r):
        return column(n["rel_ids"][r : r + 1, :], edges)

    def prepare(r):
        for side, name in enumerate(("own_neg", "far_neg")):
            n["count"][2 * r + side : 2 * r + side + 1, :] = counts(n[name][r : r + 1, :])
        if r == 0:
            table_copy.wait()
        hot = (iota((edges, nrel), 1) == rel_column(r)).astype(BF)
        rel_vec[r, :, :width] = mm(hot, n["rel_table"][...], 1, 1)

    prepare(0)
    prepare(1)
    pl.semaphore_wait(barrier, len(everyone))

    def edge_step(r):
        own, far = n["own"][r], n["far"][r]
        head_hot = (iota((touch, edges), 0) == n["heads"][r : r + 1, :]).astype(BF)
        tail_hot = (iota((touch, edges), 0) == n["tails"][r : r + 1, :]).astype(BF)
        rel = rel_vec[r]
        head_vec = mm(head_hot, own, 0, 0)
        tail_vec = mm(tail_hot, far, 0, 0)
        positive = jnp.sum(head_vec * rel * tail_vec, axis=-1, keepdims=True)
        query_tail = (head_vec * rel).astype(BF)
        query_head = (tail_vec * rel).astype(BF)
        own_count = n["count"][2 * r : 2 * r + 1, :]
        far_count = n["count"][2 * r + 1 : 2 * r + 2, :]
        weight_tail = (jax.nn.sigmoid(mm(query_tail, far, 1, 1)) * far_count).astype(BF)
        weight_head = (jax.nn.sigmoid(mm(query_head, own, 1, 1)) * own_count).astype(BF)
        back_tail = mm(weight_tail, far, 1, 0)
        back_head = mm(weight_head, own, 1, 0)
        coeff = -jax.nn.sigmoid(-positive)

        def spread(hot, grad, weight, query):
            hi = grad.astype(BF)
            lo = (grad - hi.astype(F32)).astype(BF)
            return (mm(hot, hi, 1, 0) + mm(hot, lo, 1, 0) + mm(weight, query, 0, 0)).astype(BF)

        n["own_grad"][r] = spread(head_hot, rel * (coeff * tail_vec + back_tail), weight_head, query_head)
        n["far_grad"][r] = spread(tail_hot, rel * (coeff * head_vec + back_head), weight_tail, query_tail)
        grad_rel = coeff * head_vec * tail_vec + head_vec * back_tail + tail_vec * back_head
        rows = n["rows"].at[r, 0, pl.ds(0, edges)]
        rows[:, :TAIL] = grad_rel[:, :TAIL].astype(BF)
        at, ids = iota((edges, 128), 1), rel_column(r)
        marks = jnp.where(at == MARK, ids >> 6, jnp.where(at == MARK + 1, ids & 63, 0)).astype(F32)
        rows[:, TAIL:] = jnp.where(at < width - TAIL, grad_rel[:, TAIL:], marks).astype(BF)

    def update(row_grad):
        accum = n["accum"][...] + jnp.sum(row_grad * row_grad, axis=-1, keepdims=True) * (1.0 / width)
        n["accum"][...] = accum
        emb[...] = emb[...] - LEARN_RATE * row_grad / jnp.sqrt(accum)

    def slot_rows(r, near, d):
        return n["rows"].at[r, near, pl.ds(d * edges, edges)]

    def x_copy(r, e):
        return remote(slot_rows(r, 0, 0), slot_rows(r, 0, e), n["x_send"].at[r, e], n["x_recv"].at[r, e], place.along_x(xs - e))

    def core_copy(r, d):
        return remote(slot_rows(r, 0, d), slot_rows(r, 1, d), n["core_send"].at[r, d], n["core_recv"].at[r, d], (place.mate, place.s))

    def rows_start(r):
        for e in range(1, xs):
            x_copy(r, e).start()
        core_copy(r, 0).start()

    def rows_forward(r):
        for e in range(1, xs):
            x_copy(r, e).wait_recv()
            core_copy(r, e).start()

    def rows_sum(r):
        for d in range(xs):
            core_copy(r, d).wait_recv()
        base = (place.x * INNER + place.core) * (2 * seg)
        total = n["dense"][...] if r else jnp.zeros((4 * seg, WIDE), F32)
        for near in range(2):
            block = n["rows"][r, near]
            marks = block[:, TAIL:].astype(F32)
            at = iota(marks.shape, 1)
            ids = jnp.sum(jnp.where(at == MARK, marks * 64.0, jnp.where(at == MARK + 1, marks, 0.0)), axis=1, keepdims=True)
            col = iota((xs * edges, 4 * seg), 1)
            target = base + col + jnp.where(col >= 2 * seg, 2 * seg, 0)
            total = total + mm((ids.astype(I32) == target).astype(BF), block, 0, 0)
        n["dense"][...] = total
        for e in range(1, xs):
            x_copy(r, e).wait_send()
        for d in range(xs):
            core_copy(r, d).wait_send()

    def seg_rows(ylo, yh):
        return pl.ds(pl.multiple_of((ylo * 2 + yh) * seg, seg), seg)

    def y_copy(k):
        ylo = place.ylo if k == 0 else 1 - place.ylo
        yh = place.yh if k == 1 else 1 - place.yh
        return remote(n["y_out"].at[seg_rows(ylo, yh)], n["y_in"].at[k], n["y_send"].at[k], n["y_recv"].at[k], place.peers(1)[k])

    def y_start():
        n["y_out"][...] = n["dense"][...].astype(BF)
        for k in range(3):
            y_copy(k).start()

    def z_copy(e):
        src = n["z_out"].at[lax.rem(place.z + zs - e, zs)]
        return remote(src, n["z_in"].at[e], n["z_send"].at[e], n["z_recv"].at[e], place.along_z(zs - e))

    def z_start():
        total = n["dense"][seg_rows(place.ylo, place.yh), :]
        for k in range(3):
            y_copy(k).wait_recv()
            total = total + n["y_in"][k].astype(F32)
        total = total.astype(BF)
        row, col = iota((zs * 16, seg), 0), iota((zs * 16, seg), 1)
        zz, k = row >> 4, row & 15
        packed = jnp.zeros((zs * 16, 128), F32)
        full = TAIL // 128
        for c in range(full):
            j = k - c * RELS
            hot = ((col == zz * RELS + j) & (j >= 0) & (j < RELS)).astype(BF)
            packed = packed + mm(hot, total[:, c * 128 : (c + 1) * 128], 1, 0)
        rest = width - TAIL
        last = total[:, TAIL:].astype(F32)
        last = jnp.where(iota(last.shape, 1) < rest, last, 0.0)
        for j in range(RELS):
            hot = ((col == zz * RELS + j) & (k == full * RELS)).astype(BF)
            moved = last if j == 0 else pltpu.roll(last, j * rest, 1)
            packed = packed + mm(hot, moved.astype(BF), 1, 0)
        packed = packed.astype(BF)
        for zz in range(zs):
            n["z_out"][zz] = packed[zz * 16 : (zz + 1) * 16]
        for e in range(1, zs):
            z_copy(e).start()

    def z_end():
        total = n["z_out"][place.z].astype(F32)
        for e in range(1, zs):
            z_copy(e).wait_recv()
            total = total + n["z_in"][e].astype(F32)
        share = n["share"]
        share[...] = jnp.zeros_like(share)
        full, rest = TAIL // 128, width - TAIL
        for c in range(full):
            share[:RELS, c * 128 : (c + 1) * 128] = total[c * RELS : (c + 1) * RELS, :]
        for j in range(RELS):
            last = total[full * RELS : full * RELS + 1, :]
            last = last if j == 0 else pltpu.roll(last, 128 - j * rest, 1)
            share[j : j + 1, TAIL:] = jnp.where(iota((1, 128), 1) < rest, last, 0.0)
        value = share[...]
        squares = jnp.sum(value * value, axis=-1, keepdims=True) * (1.0 / width)
        rel_accum = column(n["rel_accum"][...], value.shape[0]) + squares
        rel_accum = jnp.where(iota(rel_accum.shape, 0) < RELS, rel_accum, 1.0)
        value = -LEARN_RATE * value / jnp.sqrt(rel_accum)
        n["step_out"][...] = value[:RELS, :width]
        n["rel_accum_out"][...] = as_row(rel_accum, RELS)
        for k in range(3):
            y_copy(k).wait_send()
        for e in range(1, zs):
            z_copy(e).wait_send()

    last_step = zs // 2
    for r in range(2):
        if r:
            write_block(r)
        fetch(
            place, r, slot, n["block"].at[r], n["line"].at[r], n["picked"].at[r], n["own"].at[r], n["far"].at[r], n["idx"].at[r],
            Ring(place, n["f_send"].at[r], n["f_recv"].at[r]), n["fp_send"].at[r], n["fp_recv"].at[r], n["f_self"].at[r],
            {0: functools.partial(rows_sum, 0)} if r else {},
        )
        edge_step(r)
        steps = {0: [functools.partial(rows_start, r)]}
        plan = ((2, functools.partial(rows_forward, r)),)
        if r:
            plan = plan + ((4, functools.partial(rows_sum, r)), (4, y_start), (6, z_start))
        for t, what in plan:
            steps.setdefault(min(t, last_step), []).append(what)
        aside = {t: (lambda todo=todo: [f() for f in todo]) for t, todo in steps.items()}
        row_grad = give_back(
            place, r, slot, n["own_grad"].at[r], n["far_grad"].at[r], n["idx"].at[r], n["got"].at[r], n["term"], n["sent"].at[r], n["came"].at[r],
            Ring(place, n["s_send"].at[r], n["s_recv"].at[r]), n["sp_send"].at[r], n["sp_recv"].at[r], n["s_self"].at[r], aside,
        )
        update(row_grad)
    n["emb_out"][...] = emb[:, :width]
    n["accum_out"][...] = as_row(n["accum"][...], PER)
    z_end()


def run(inputs, zs, xs, slot):
    width = inputs["emb_in"].shape[1]
    touch = 2 * zs * slot
    edges = inputs["heads"].shape[1]
    half = zs // 2
    seg = zs * RELS
    dma = pltpu.SemaphoreType.DMA
    vmem = pltpu.VMEM
    outputs = dict(
        emb_out=jax.ShapeDtypeStruct((PER, width), F32),
        accum_out=jax.ShapeDtypeStruct((1, PER), F32),
        step_out=jax.ShapeDtypeStruct((RELS, width), F32),
        rel_accum_out=jax.ShapeDtypeStruct((1, RELS), F32),
    )
    scratch = dict(
        emb=vmem((PER, WIDE), F32),
        rel_table=vmem(inputs["relations"].shape, BF),
        accum=vmem((PER, 1), F32),
        share=vmem((8, WIDE), F32),
        rel_vec=vmem((2, edges, WIDE), F32),
        count=vmem((4, touch), F32),
        block=vmem((2, PACKED, 128), BF),
        line=vmem((2, zs, PACKED, 128), BF),
        picked=vmem((2, zs, PER, WIDE), BF),
        own=vmem((2, touch, WIDE), BF),
        far=vmem((2, touch, WIDE), BF),
        idx=vmem((2, zs, 128), F32),
        own_grad=vmem((2, touch, WIDE), BF),
        far_grad=vmem((2, touch, WIDE), BF),
        got=vmem((2, zs, PER, WIDE), BF),
        term=vmem((zs, PACKED, 128), F32),
        sent=vmem((2, 2, half, PACKED, 128), BF),
        came=vmem((2, 2, half, PACKED, 128), BF),
        rows=vmem((2, 2, xs * edges, WIDE), BF),
        dense=vmem((4 * seg, WIDE), F32),
        y_out=vmem((4 * seg, WIDE), BF),
        y_in=vmem((3, seg, WIDE), BF),
        z_out=vmem((zs, 16, 128), BF),
        z_in=vmem((zs, 16, 128), BF),
        table_sem=dma,
        f_send=dma((2, 2, half, 2)),
        f_recv=dma((2, 2, half, 2)),
        fp_send=dma((2, 3)),
        fp_recv=dma((2, 3)),
        f_self=dma((2,)),
        s_send=dma((2, 2, half, 2)),
        s_recv=dma((2, 2, half, 2)),
        sp_send=dma((2, 3)),
        sp_recv=dma((2, zs, 3)),
        s_self=dma((2, zs)),
        x_send=dma((2, xs)),
        x_recv=dma((2, xs)),
        core_send=dma((2, xs)),
        core_recv=dma((2, xs)),
        y_send=dma((3,)),
        y_recv=dma((3,)),
        z_send=dma((zs,)),
        z_recv=dma((zs,)),
    )
    in_vmem = pl.BlockSpec(memory_space=pltpu.VMEM)
    names = (*inputs, *outputs, *scratch)
    return pl.pallas_call(
        functools.partial(main_kernel, zs, xs, slot, width, names),
        name="train_step",
        out_shape=tuple(outputs.values()),
        in_specs=[pl.BlockSpec(memory_space=pl.ANY) if k == "relations" else in_vmem for k in inputs],
        out_specs=(in_vmem,) * len(outputs),
        scratch_shapes=list(scratch.values()),
        compiler_params=pltpu.CompilerParams(collective_id=0, has_side_effects=True),
    )(*inputs.values())


def finish_kernel(*refs):
    half = len(refs) // 2
    for src, dst in zip(refs[:half], refs[half:]):
        dst[...] = src[...]


def finish(*values):
    in_vmem = pl.BlockSpec(memory_space=pltpu.VMEM)
    return pl.pallas_call(
        finish_kernel,
        name="finish",
        out_shape=tuple(jax.ShapeDtypeStruct(v.shape, v.dtype) for v in values),
        in_specs=[in_vmem] * len(values),
        out_specs=(in_vmem,) * len(values),
    )(*values)


def body(embeddings, row_accum, relations, relation_accum, request_rows, head_slots, tail_slots, relation_ids, own_negatives, far_negatives):
    rounds, shards, sides, slot = request_rows.shape
    inputs = dict(
        emb_in=embeddings,
        accum_in=row_accum[None, :],
        relations=relations.T,
        rel_accum=relation_accum[None, :],
        requests=request_rows.transpose(0, 2, 3, 1).reshape(rounds, sides * slot, shards),
        heads=head_slots,
        tails=tail_slots,
        rel_ids=relation_ids,
        own_neg=own_negatives,
        far_neg=far_negatives,
    )
    emb, accum, step, rel_accum = finish(*run(inputs, shards // 2, lax.axis_size("dom") // INNER, slot))
    return (emb, accum[0], step, rel_accum[0])


def solution(mesh):
    both = ("dom", "shard")
    return jax.shard_map(
        body,
        mesh=mesh,
        in_specs=(P(both, None), P(both), P(), P(both), P(None, both, None, None)) + (P(None, both),) * 5,
        out_specs=(P(both, None), P(both), P(both, None), P(both)),
        check_vma=False,
    )
```
